32 devices in a mesh: grp: 2 (over y), ex: 4 (over z), col: 4 (over x, core).
Axes of the slice: x: 2, y: 2, z: 4, core: 2. Of those that a mesh axis runs over, the one named last changes fastest.
Arguments:
- hidden_input: bfloat16 [8, 2, 256, 5120], P(('grp', 'ex'), None, None, 'col'), parts along dimension 0, may hold values from -6 to 6
- output_gradient: bfloat16 [8, 2, 256, 5120], P(('grp', 'ex'), None, None, 'col'), parts along dimension 0, may hold values from -11 to 11
- lengths: int32 [8], P(('grp', 'ex')), parts along dimension 0, may hold values from 64 to 256
- adapter_down: bfloat16 [2, 128, 5120], P(None, None, 'col'), may hold values from -0.078125 to 0.078125
- adapter_up: bfloat16 [2, 5120, 128], P(None, 'col'), may hold values from -0.078125 to 0.078125
- left_sign_words: int32 [2, 2, 32, 5120], P(None, None, None, 'col'), may hold values from 0 to 65535
- right_sign_words: int32 [2, 2, 128, 4], replicated, may hold values from 0 to 1
- targets: float32 [512, 8192], P(('grp', 'ex'), 'col'), parts along dimension 0, may hold values from -40 to 40
Outputs:
- gradient_features: float32 [8, 8192], P(('grp', 'ex'), 'col'), parts along dimension 0
- scores: float32 [8, 256], P(('grp', 'ex'), 'col'), parts along dimension 0
The draws below stay inside these ranges and needn't reach their ends.
There are 2 independent parts, one for each index of `grp`. The reference program is written for one: setup_inputs(seed, part) draws one part's arguments, and reference() takes and returns one part's arrays. A program takes and returns all parts, laid end to end along the dimension named above; an argument that names none is the same for every part. Nothing has to cross between parts.
Inputs may be any that keep to these rules, and one draw needn't show every extreme that they name: `left_sign_words`: each word holds 16 independent bits.
All inputs are finite; a program needn't handle non-finite values.
Results may differ from the reference program's by a relative error of at most 0.0003.
Values sent between devices are 32-bit elements; how exact they have to be, the bound alone decides.
A program may use at most 64 MiB of HBM per device.

```python
import math
import jax
import jax.numpy as jnp
from jax import lax

MODEL_WIDTH = 5120
ADAPTER_RANK = 128
SEQ = 256
ADAPTED_LAYERS = 2
K_LEFT = 512
M_RIGHT = 4
TARGETS = 256
CANDS = 4
COLS = 8192


def draw_output_gradient(key, part):
    shape_all = (CANDS, ADAPTED_LAYERS, SEQ, MODEL_WIDTH)
    levels = jnp.arange(ADAPTED_LAYERS, dtype=jnp.float32) / max(ADAPTED_LAYERS - 1, 1)
    values = jnp.clip(jax.random.normal(key, shape_all, jnp.float32), -6.0, 6.0)
    scales = 3.0 ** (0.5 * levels)
    return (values * scales[None, :, None, None]).astype(jnp.bfloat16)


def draw_targets(key, part):
    column_pos = jnp.arange(COLS, dtype=jnp.float32) / (COLS - 1)
    values = jnp.clip(jax.random.normal(key, (TARGETS, COLS), jnp.float32), -6.0, 6.0)
    return values * (3.0 ** (0.5 * column_pos))[None, :]


def with_ends(values, rng, least, top_value):
    longest = values.shape.index(max(values.shape))
    spots = []
    for shift in (0, 1):
        where = [jax.random.randint(jax.random.fold_in(rng, axis), (), 0, length) for axis, length in enumerate(values.shape)]
        where[longest] = (where[longest] + shift) % values.shape[longest]
        spots.append(tuple(where))
    return values.at[spots[0]].set(least).at[spots[1]].set(top_value)


def level_of(stream_key, dims, shards, low, largest):
    gain, own = 1.0, jax.random.fold_in(stream_key, 6)
    for axis_at, blocks in shards:
        heights = jnp.exp(jax.random.uniform(jax.random.fold_in(own, axis_at), (blocks,), jnp.float32, low / len(shards), largest / len(shards)))
        gain = gain * jnp.repeat(heights, dims[axis_at] // blocks).reshape([-1 if axis == axis_at else 1 for axis in range(len(dims))])
    return gain


def gaussian(rng, shape, spread, bound, cuts=(), held_as=jnp.bfloat16):
    gain = level_of(rng, shape, cuts, -0.22, 0.18) if cuts else 1.0
    result = jax.random.normal(rng, shape, jnp.float32) * spread * gain
    return jnp.minimum(jnp.maximum(result, -bound), bound).astype(held_as)


def setup_inputs(seed: int = 0, part: int = 0) -> dict:
    splits = jax.random.split(jax.random.key(seed), 9)
    part_splits = jax.random.split(jax.random.fold_in(splits[8], part), 9)
    hidden_input = gaussian(part_splits[0], (CANDS, ADAPTED_LAYERS, SEQ, MODEL_WIDTH), 1.0, 6.0, ((0, 4), (3, 4)))
    output_gradient = draw_output_gradient(jax.random.fold_in(jax.random.fold_in(splits[8], part), 71), part)
    lengths = with_ends(jax.random.randint(part_splits[2], (CANDS,), SEQ // 4, SEQ + 1), jax.random.fold_in(part_splits[2], 1), SEQ // 4, SEQ).astype(jnp.int32)
    adapter_down = gaussian(splits[3], (ADAPTED_LAYERS, ADAPTER_RANK, MODEL_WIDTH), MODEL_WIDTH ** -0.5, 0.078125, ((2, 4),))
    adapter_up = gaussian(splits[4], (ADAPTED_LAYERS, MODEL_WIDTH, ADAPTER_RANK), MODEL_WIDTH ** -0.5, 0.078125, ((1, 4),))
    left_sign_words = with_ends(jax.random.randint(splits[5], (ADAPTED_LAYERS, 2, K_LEFT // 16, MODEL_WIDTH), 0, 65536), jax.random.fold_in(splits[5], 1), 0, 65535).astype(jnp.int32)
    right_sign_words = with_ends(jax.random.randint(splits[6], (ADAPTED_LAYERS, 2, ADAPTER_RANK, M_RIGHT), 0, 2), jax.random.fold_in(splits[6], 1), 0, 1).astype(jnp.int32)
    targets = draw_targets(jax.random.fold_in(jax.random.fold_in(splits[8], part), 71), part)
    return {"hidden_input": hidden_input, "output_gradient": output_gradient, "lengths": lengths, "adapter_down": adapter_down, "adapter_up": adapter_up, "left_sign_words": left_sign_words, "right_sign_words": right_sign_words, "targets": targets}


epsilon = 1e-06
highest_precision = lax.Precision.HIGHEST

def unpack(packed):
    shifts = jnp.arange(16, dtype=jnp.int32)
    bit_values = jnp.right_shift(packed[..., :, None, :], shifts[:, None]) & 1
    shape_out = packed.shape[:-2] + (packed.shape[-2] * 16, packed.shape[-1])
    return (2 * bit_values - 1).reshape(shape_out)

def reference(hidden_input, output_gradient, lengths, adapter_down, adapter_up, left_sign_words, right_sign_words, targets):
    positions = jnp.arange(SEQ, dtype=jnp.int32)
    token_weights = jnp.where(positions[None, :] < lengths[:, None], 1.0, 0.0).astype(jnp.float32) / lengths[:, None].astype(jnp.float32)
    left_signs = unpack(left_sign_words).astype(jnp.float32)
    right_signs = (2 * right_sign_words - 1).astype(jnp.float32)
    blocks = []
    for index_of_layer in range(ADAPTED_LAYERS):
        input_rows = hidden_input[:, index_of_layer].astype(jnp.float32)
        gradient_value = output_gradient[:, index_of_layer].astype(jnp.float32)
        shrunk_input = jnp.einsum('aom,cm->aoc', input_rows, adapter_down[index_of_layer].astype(jnp.float32), precision=highest_precision)
        shrunk_gradient = jnp.einsum('wvl,lz->wvz', gradient_value, adapter_up[index_of_layer].astype(jnp.float32), precision=highest_precision)
        mixed_b = jnp.einsum('esr,rm->esm', shrunk_input, right_signs[index_of_layer, 0], precision=highest_precision) * token_weights[:, :, None]
        mixed_a = jnp.einsum('esr,rm->esm', shrunk_gradient, right_signs[index_of_layer, 1], precision=highest_precision) * token_weights[:, :, None]
        signed_grad = jnp.einsum('esd,kd->esk', gradient_value, left_signs[index_of_layer, 0], precision=highest_precision)
        signed_input = jnp.einsum('esd,kd->esk', input_rows, left_signs[index_of_layer, 1], precision=highest_precision)
        block_b = jnp.einsum('esm,esk->emk', mixed_b, signed_grad, precision=highest_precision)
        block_a = jnp.einsum('esm,esk->emk', mixed_a, signed_input, precision=highest_precision)
        blocks.append(jnp.stack([block_b, block_a], axis=1))
    sketch = jnp.stack(blocks, axis=1).reshape(CANDS, COLS)
    cand_squares = lax.optimization_barrier(jnp.sum(sketch * sketch, axis=1))
    gradient_features = sketch * lax.rsqrt(cand_squares / COLS + epsilon)[:, None]
    target_squares = lax.optimization_barrier(jnp.sum(targets * targets, axis=1))
    target_units = targets * lax.rsqrt(target_squares / COLS + epsilon)[:, None]
    scores = jnp.dot(gradient_features, target_units.T, precision=highest_precision) / math.sqrt(COLS)
    return (gradient_features, scores)
```

```python
import functools
import math

import jax
import jax.numpy as jnp
from jax import lax
from jax.experimental import pallas as pl
from jax.experimental.pallas import tpu as pltpu
from jax.sharding import PartitionSpec as P

MESH = pl.DeviceIdType.MESH
F32 = jnp.float32
BF16 = jnp.bfloat16
BITS = 16
epsilon = 1e-06


def nt(a, b):
    return lax.dot_general(a, b, (((1,), (1,)), ((), ())), preferred_element_type=F32)


def halves(x):
    high = x.astype(BF16).astype(F32)
    return jnp.concatenate([high, x - high], axis=0).astype(BF16)


def repeat(count, body):
    if count <= 8:
        for i in range(count):
            body(i)
    else:

        def step(i, carry):
            body(i)
            return carry

        lax.fori_loop(0, count, step, 0)


def kernel(
    nex,
    ncol,
    groups,
    h_hbm,
    g_hbm,
    len_ref,
    down_hbm,
    up_hbm,
    words_hbm,
    right_hbm,
    tg_hbm,
    out_ref,
    h_ref,
    g_ref,
    down_ref,
    up_ref,
    words_ref,
    right_ref,
    tg_ref,
    signs_ref,
    st_hi_ref,
    st_lo_ref,
    t_ref,
    fold_ref,
    mix_ref,
    mix_in_ref,
    tsq_ref,
    tsq_in_ref,
    sk_ref,
    rx_ref,
    ps_ref,
    fin_ref,
    load_sem,
    ready_sem,
    mix_ssem,
    mix_rsem,
    tsq_ssem,
    tsq_rsem,
    sk_ssem,
    sk_rsem,
    ps_ssem,
    fin_rsem,
):
    ie, ic = lax.axis_index("ex"), lax.axis_index("col")
    layers = h_ref.shape[0]
    seq = h_ref.shape[1]
    m_right = right_ref.shape[2]
    nwords = words_ref.shape[2]
    width = words_ref.shape[3]
    k_left = nwords * BITS
    tpd = tg_ref.shape[0]
    cols = tg_ref.shape[1] * ncol
    rows = rx_ref.shape[2]
    members = nex * ncol

    def load(n, src, dst):
        return pltpu.make_async_copy(src, dst, load_sem.at[n])

    words_load = load(0, words_hbm, words_ref)
    right_load = load(1, right_hbm, right_ref)
    down_load = load(2, down_hbm, down_ref)
    up_load = load(3, up_hbm, up_ref)
    h_loads = [load(4 + 2 * l, h_hbm.at[0, l], h_ref.at[l]) for l in range(layers)]
    g_loads = [load(5 + 2 * l, g_hbm.at[0, l], g_ref.at[l]) for l in range(layers)]
    tg_load = load(4 + 2 * layers, tg_hbm, tg_ref)
    right_load.start()
    down_load.start()
    up_load.start()
    for l in range(layers):
        h_loads[l].start()
        g_loads[l].start()
    words_load.start()
    tg_load.start()

    barrier = pltpu.get_barrier_semaphore()
    me = ie * ncol + ic

    def signal(semaphore, other):
        pl.semaphore_signal(
            semaphore,
            inc=1,
            device_id={"ex": other // ncol, "col": lax.rem(other, ncol)},
            device_id_type=MESH,
        )

    def greet(other, carry):
        @pl.when(other != me)
        def _():
            signal(barrier, other)

        return carry

    lax.fori_loop(ie * ncol, members, greet, 0)

    def answer(other, carry):
        signal(ready_sem, other)
        return carry

    def col_copy(src, dst, ssem, rsem, step):
        return pltpu.make_async_remote_copy(
            src_ref=src,
            dst_ref=dst,
            send_sem=ssem,
            recv_sem=rsem,
            device_id={"col": lax.rem(ic + step, ncol)},
            device_id_type=MESH,
        )

    right_load.wait()
    down_load.wait()
    up_load.wait()
    for l in range(layers):
        for j in range(2):
            right_t = (2 * right_ref[l, j] - 1).astype(F32).astype(BF16)
            if j == 0:
                folded = jnp.dot(right_t, down_ref[l], preferred_element_type=F32)
            else:
                folded = nt(right_t, up_ref[l])
            fold_ref[2 * l + j] = halves(folded)

    mix_copies = [[] for _ in range(layers)]
    for l in range(layers):
        h_loads[l].wait()
        g_loads[l].wait()
        for j in range(2):
            both = nt(fold_ref[2 * l + j], h_ref[l] if j == 0 else g_ref[l])
            mix_ref[l, j] = both[:m_right] + both[m_right:]
        if l == 0:
            pl.semaphore_wait(barrier, ncol - 1 + ie * ncol)
        for step in range(1, ncol):
            copy = col_copy(
                mix_ref.at[l],
                mix_in_ref.at[step - 1, l],
                mix_ssem.at[step - 1, l],
                mix_rsem.at[step - 1, l],
                step,
            )
            copy.start()
            mix_copies[l].append(copy)
    lax.fori_loop(0, ie * ncol, answer, 0)

    tg_load.wait()
    targets = tg_ref[...]
    high = targets.astype(BF16)
    t_ref[0:tpd] = high
    t_ref[tpd : 2 * tpd] = (targets - high.astype(F32)).astype(BF16)
    squares = targets * targets
    lanes = 128
    folded = squares[:, 0:lanes]
    for b in range(1, squares.shape[1] // lanes):
        folded = folded + squares[:, b * lanes : (b + 1) * lanes]
    sq_high = folded.astype(BF16)
    rest = folded - sq_high.astype(F32)
    sq_mid = rest.astype(BF16)
    sq_low = (rest - sq_mid.astype(F32)).astype(BF16)
    ones = jnp.ones((8, lanes), BF16)
    row = (nt(ones, sq_high) + nt(ones, sq_mid) + nt(ones, sq_low))[0:1]
    tsq_ref[...] = jnp.zeros_like(tsq_ref)
    tsq_ref[:, 0:tpd] = row
    tsq_copies = []
    for step in range(1, ncol):
        copy = col_copy(
            tsq_ref, tsq_in_ref.at[step - 1], tsq_ssem.at[step - 1], tsq_rsem.at[step - 1], step
        )
        copy.start()
        tsq_copies.append(copy)

    words_load.wait()
    row_bit = jnp.left_shift(1, lax.broadcasted_iota(jnp.int32, (BITS, width), 0))

    def unpack(n):
        for w in range(nwords):
            word = words_ref[n // 2, n % 2, w : w + 1, :]
            bits = jnp.bitwise_and(jnp.broadcast_to(word, (BITS, width)), row_bit)
            signs_ref[n, w * BITS : (w + 1) * BITS, :] = jnp.where(bits != 0, 1.0, -1.0).astype(BF16)

    unpack(0)
    for n in range(2 * layers):
        if n + 1 < 2 * layers:
            unpack(n + 1)
        st = nt(signs_ref[n], g_ref[n // 2] if n % 2 == 0 else h_ref[n // 2])
        st_high = st.astype(BF16)
        st_hi_ref[n] = st_high
        st_lo_ref[n] = (st - st_high.astype(F32)).astype(BF16)
    ps_ref[...] = jnp.zeros_like(ps_ref)

    length = len_ref[0]
    position = lax.broadcasted_iota(jnp.int32, (1, seq), 1)
    weights = jnp.where(position < length, 1.0, 0.0).astype(F32) / jnp.full(
        (1, seq), length, jnp.int32
    ).astype(F32)
    for copies in mix_copies:
        for copy in copies:
            copy.wait_recv()
    for l in range(layers):
        total = mix_ref[l]
        for step in range(1, ncol):
            total = total + mix_in_ref[step - 1, l]
        left = halves(jnp.concatenate([total[0], total[1]], axis=0) * weights)
        for j in range(2):
            n = 2 * l + j
            out = nt(left, st_hi_ref[n]) + nt(left, st_lo_ref[n])
            half = out.shape[0] // 2
            out = out[:half] + out[half:]
            at = n * m_right
            sk_ref[at // rows, at % rows : at % rows + m_right, :] = out[
                j * m_right : (j + 1) * m_right
            ]

    def block_copy(row, ssem_at, block):
        return pltpu.make_async_remote_copy(
            src_ref=sk_ref.at[block],
            dst_ref=rx_ref.at[ie, ic],
            send_sem=sk_ssem.at[ssem_at, block],
            recv_sem=sk_rsem.at[ie, ic],
            device_id={"ex": row, "col": block},
            device_id_type=MESH,
        )

    own_blocks = [lax.rem(ic + step, ncol) for step in range(1, ncol)]
    for block in own_blocks:
        block_copy(ie, nex - 1, block).start()
    pltpu.make_async_copy(sk_ref.at[ic], rx_ref.at[ie, ic], sk_rsem.at[ie, ic]).start()

    @pl.when(ie < nex - 1)
    def _():
        pl.semaphore_wait(ready_sem, (nex - 1 - ie) * ncol)

    def other_row(i):
        return i + jnp.where(i >= ie, 1, 0)

    def send_row(i):
        for block in range(ncol):
            block_copy(other_row(i), i, block).start()

    repeat(nex - 1, send_row)

    tsq = tsq_ref[...]
    for step in range(1, ncol):
        tsq_copies[step - 1].wait_recv()
        tsq = tsq + tsq_in_ref[step - 1]
    t_scale = (lax.rsqrt(tsq / cols + epsilon) / math.sqrt(cols))[:, 0:tpd]

    goal = ie // groups
    slot = lax.rem(ie, groups) * ncol + ic

    def score_copy(e):
        return pltpu.make_async_remote_copy(
            src_ref=ps_ref.at[e],
            dst_ref=fin_ref.at[slot],
            send_sem=ps_ssem.at[e],
            recv_sem=fin_rsem.at[slot],
            device_id={"ex": e, "col": goal},
            device_id_type=MESH,
        )

    def candidate(e):
        total = rx_ref[e, 0]
        for c in range(1, ncol):
            total = total + rx_ref[e, c]
        return total

    def stays(e):
        return jnp.logical_and(e == ie, goal == ic)

    def score(e):
        for c in range(ncol):
            pltpu.make_async_remote_copy(
                src_ref=sk_ref.at[0],
                dst_ref=rx_ref.at[e, c],
                send_sem=sk_ssem.at[0, 0],
                recv_sem=sk_rsem.at[e, c],
                device_id={"ex": ie, "col": ic},
                device_id_type=MESH,
            ).wait_recv()
        total = candidate(e)
        part = jnp.zeros((2, 2 * tpd), F32)
        for r in range(rows):
            part = part + nt(halves(total[r : r + 1]), t_ref[:, r * k_left : (r + 1) * k_left])
        part = part[0:1] + part[1:2]
        part = (part[:, 0:tpd] + part[:, tpd : 2 * tpd]) * t_scale
        if groups > 1:
            where = lax.rem(ie, groups) * tpd
            place = (
                lax.broadcasted_iota(jnp.int32, (tpd, tpd * groups), 0) + where
                == lax.broadcasted_iota(jnp.int32, (tpd, tpd * groups), 1)
            ).astype(F32)
            part = jnp.dot(
                part, place, precision=lax.Precision.HIGHEST, preferred_element_type=F32
            )
        squares = jnp.sum(jnp.sum(total * total, axis=1, keepdims=True), axis=0, keepdims=True)
        ps_ref[e, 0:1, 0 : part.shape[1]] = part
        ps_ref[e, 1:2, :] = jnp.broadcast_to(squares, (1, 128))

        @pl.when(jnp.logical_not(stays(e)))
        def _():
            score_copy(e).start()

        @pl.when(stays(e))
        def _():
            pltpu.make_async_copy(ps_ref.at[e], fin_ref.at[slot], fin_rsem.at[slot]).start()

    repeat(nex, score)

    own = candidate(ie)
    for copies in mix_copies + [tsq_copies]:
        for copy in copies:
            copy.wait_send()
    for block in own_blocks:
        block_copy(ie, nex - 1, block).wait_send()

    def drain_row(i):
        for block in range(ncol):
            block_copy(other_row(i), i, block).wait_send()

    repeat(nex - 1, drain_row)

    for k in range(groups * ncol):
        pltpu.make_async_remote_copy(
            src_ref=ps_ref.at[0],
            dst_ref=fin_ref.at[k],
            send_sem=ps_ssem.at[0],
            recv_sem=fin_rsem.at[k],
            device_id={"ex": ie, "col": ic},
            device_id_type=MESH,
        ).wait_recv()

    result = fin_ref[0, 0:1]
    for k in range(1, groups * ncol):
        result = result + fin_ref[k, 0:1]
    csq = fin_ref[0, 1:2]
    for k in range(1, ncol):
        csq = csq + fin_ref[k, 1:2]
    c_scale = lax.rsqrt(csq / cols + epsilon)
    own_scale = jnp.concatenate([c_scale] * (k_left // 128), axis=1)
    out_ref[0:rows] = own * own_scale
    out_ref[rows : rows + 1, 0:128] = result * c_scale

    def drain_score(e):
        @pl.when(jnp.logical_not(stays(e)))
        def _():
            score_copy(e).wait_send()

    repeat(nex, drain_score)


def spread(packed_ref, feat_ref, score_ref):
    rows = packed_ref.shape[0] // 2
    k_left = packed_ref.shape[1]
    for r in range(rows):
        feat_ref[:, r * k_left : (r + 1) * k_left] = packed_ref[r : r + 1]
    score_ref[...] = packed_ref[rows : rows + 1, 0 : score_ref.shape[1]]


def on_device(
    nex,
    ncol,
    hidden_input,
    output_gradient,
    lengths,
    adapter_down,
    adapter_up,
    left_sign_words,
    right_sign_words,
    targets,
):
    examples, layers, seq, width = hidden_input.shape
    right_by_column = jnp.swapaxes(right_sign_words, 2, 3)
    nwords = left_sign_words.shape[2]
    m_right = right_sign_words.shape[3]
    k_left = nwords * BITS
    tpd, own_cols = targets.shape
    rows = own_cols // k_left
    groups = nex // ncol
    assert examples == 1 and nex == groups * ncol and rows * k_left == own_cols
    assert rows % m_right == 0 and rows * ncol == layers * 2 * m_right
    blocks = 2 * layers
    span = tpd * groups
    any_space = pl.BlockSpec(memory_space=pltpu.HBM)
    vmem = pl.BlockSpec(memory_space=pltpu.VMEM)
    peers = ncol - 1
    sems = pltpu.SemaphoreType.DMA
    packed = pl.pallas_call(
        functools.partial(kernel, nex, ncol, groups),
        out_shape=pltpu.VMEM((2 * rows, k_left), F32),
        in_specs=[any_space] * 2 + [pl.BlockSpec(memory_space=pltpu.SMEM)] + [any_space] * 5,
        out_specs=vmem,
        scratch_shapes=[
            pltpu.VMEM((layers, seq, width), BF16),
            pltpu.VMEM((layers, seq, width), BF16),
            pltpu.VMEM(adapter_down.shape, BF16),
            pltpu.VMEM(adapter_up.shape, BF16),
            pltpu.VMEM(left_sign_words.shape, jnp.int32),
            pltpu.VMEM(right_by_column.shape, jnp.int32),
            pltpu.VMEM(targets.shape, F32),
            pltpu.VMEM((blocks, k_left, width), BF16),
            pltpu.VMEM((blocks, k_left, seq), BF16),
            pltpu.VMEM((blocks, k_left, seq), BF16),
            pltpu.VMEM((2 * tpd, own_cols), BF16),
            pltpu.VMEM((blocks, 2 * m_right, width), BF16),
            pltpu.VMEM((layers, 2, m_right, seq), F32),
            pltpu.VMEM((peers, layers, 2, m_right, seq), F32),
            pltpu.VMEM((1, 128), F32),
            pltpu.VMEM((peers, 1, 128), F32),
            pltpu.VMEM((ncol, rows, k_left), F32),
            pltpu.VMEM((nex, ncol, rows, k_left), F32),
            pltpu.VMEM((nex, 2, 128), F32),
            pltpu.VMEM((groups * ncol, 2, 128), F32),
            sems((5 + 2 * layers,)),
            pltpu.SemaphoreType.REGULAR,
            sems((peers, layers)),
            sems((peers, layers)),
            sems((peers,)),
            sems((peers,)),
            sems((nex, ncol)),
            sems((nex, ncol)),
            sems((nex,)),
            sems((groups * ncol,)),
        ],
        compiler_params=pltpu.CompilerParams(collective_id=0, has_side_effects=True),
    )(
        hidden_input,
        output_gradient,
        lengths,
        adapter_down,
        adapter_up,
        left_sign_words,
        right_by_column,
        targets,
    )
    return pl.pallas_call(
        spread,
        out_shape=(
            jax.ShapeDtypeStruct((1, own_cols), F32),
            jax.ShapeDtypeStruct((1, span), F32),
        ),
        in_specs=[vmem],
        out_specs=(vmem, vmem),
    )(pltpu.with_memory_space_constraint(packed, pltpu.VMEM))


def solution(mesh):
    return jax.shard_map(
        functools.partial(on_device, mesh.shape["ex"], mesh.shape["col"]),
        mesh=mesh,
        in_specs=(
            P(("grp", "ex"), None, None, "col"),
            P(("grp", "ex"), None, None, "col"),
            P(("grp", "ex")),
            P(None, None, "col"),
            P(None, "col", None),
            P(None, None, None, "col"),
            P(),
            P(("grp", "ex"), "col"),
        ),
        out_specs=(P(("grp", "ex"), "col"), P(("grp", "ex"), "col")),
        check_vma=False,
    )
```

```python
import functools
import math

import jax
import jax.numpy as jnp
from jax import lax
from jax.experimental import pallas as pl
from jax.experimental.pallas import tpu as pltpu
from jax.sharding import PartitionSpec as P

MESH = pl.DeviceIdType.MESH
F32 = jnp.float32
BF16 = jnp.bfloat16
BITS = 16
epsilon = 1e-06


def nt(a, b):
    return lax.dot_general(a, b, (((1,), (1,)), ((), ())), preferred_element_type=F32)


def halves(x):
    high = x.astype(BF16).astype(F32)
    return jnp.concatenate([high, x - high], axis=0).astype(BF16)


def repeat(count, body):
    if count <= 8:
        for i in range(count):
            body(i)
    else:

        def step(i, carry):
            body(i)
            return carry

        lax.fori_loop(0, count, step, 0)


def kernel(
    nex,
    ncol,
    groups,
    h_hbm,
    g_hbm,
    len_ref,
    down_hbm,
    up_hbm,
    words_hbm,
    right_hbm,
    tg_hbm,
    out_ref,
    h_ref,
    g_ref,
    down_ref,
    up_ref,
    words_ref,
    right_ref,
    tg_ref,
    signs_ref,
    st_hi_ref,
    st_lo_ref,
    t_ref,
    fold_ref,
    mix_ref,
    mix_in_ref,
    tsq_ref,
    tsq_in_ref,
    sk_ref,
    rx_ref,
    ps_ref,
    fin_ref,
    load_sem,
    ready_sem,
    mix_ssem,
    mix_rsem,
    tsq_ssem,
    tsq_rsem,
    own_ssem,
    sk_ssem,
    sk_rsem,
    ps_ssem,
    fin_rsem,
):
    ie, ic = lax.axis_index("ex"), lax.axis_index("col")
    layers = h_ref.shape[0]
    seq = h_ref.shape[1]
    m_right = right_ref.shape[2]
    nwords = words_ref.shape[2]
    width = words_ref.shape[3]
    k_left = nwords * BITS
    tpd = tg_ref.shape[0]
    cols = tg_ref.shape[1] * ncol
    rows = rx_ref.shape[2]
    members = nex * ncol

    def load(n, src, dst):
        return pltpu.make_async_copy(src, dst, load_sem.at[n])

    words_load = load(0, words_hbm, words_ref)
    right_load = load(1, right_hbm, right_ref)
    down_load = load(2, down_hbm, down_ref)
    up_load = load(3, up_hbm, up_ref)
    h_loads = [load(4 + 2 * l, h_hbm.at[0, l], h_ref.at[l]) for l in range(layers)]
    g_loads = [load(5 + 2 * l, g_hbm.at[0, l], g_ref.at[l]) for l in range(layers)]
    tg_load = load(4 + 2 * layers, tg_hbm, tg_ref)
    right_load.start()
    down_load.start()
    up_load.start()
    for l in range(layers):
        h_loads[l].start()
        g_loads[l].start()
    words_load.start()
    tg_load.start()

    barrier = pltpu.get_barrier_semaphore()
    me = ie * ncol + ic

    def signal(semaphore, other):
        pl.semaphore_signal(
            semaphore,
            inc=1,
            device_id={"ex": other // ncol, "col": lax.rem(other, ncol)},
            device_id_type=MESH,
        )

    def greet(other, carry):
        @pl.when(other != me)
        def _():
            signal(barrier, other)

        return carry

    lax.fori_loop(ie * ncol, members, greet, 0)

    def answer(other, carry):
        signal(ready_sem, other)
        return carry

    def col_copy(src, dst, ssem, rsem, step):
        return pltpu.make_async_remote_copy(
            src_ref=src,
            dst_ref=dst,
            send_sem=ssem,
            recv_sem=rsem,
            device_id={"col": lax.rem(ic + step, ncol)},
            device_id_type=MESH,
        )

    def passing(buffer, semaphore):
        return pltpu.make_async_remote_copy(
            src_ref=buffer,
            dst_ref=buffer,
            send_sem=semaphore,
            recv_sem=semaphore,
            device_id={"col": ic},
            device_id_type=MESH,
        )

    right_load.wait()
    down_load.wait()
    up_load.wait()
    for l in range(layers):
        for j in range(2):
            right_t = (2 * right_ref[l, j] - 1).astype(F32).astype(BF16)
            if j == 0:
                folded = jnp.dot(right_t, down_ref[l], preferred_element_type=F32)
            else:
                folded = nt(right_t, up_ref[l])
            fold_ref[2 * l + j] = halves(folded)

    for l in range(layers):
        h_loads[l].wait()
        g_loads[l].wait()
        for j in range(2):
            both = nt(fold_ref[2 * l + j], h_ref[l] if j == 0 else g_ref[l])
            mix_ref[l, j] = both[:m_right] + both[m_right:]
        if l == 0:
            pl.semaphore_wait(barrier, ncol - 1 + ie * ncol)
        for step in range(1, ncol):
            copy = col_copy(
                mix_ref.at[l],
                mix_in_ref.at[step - 1, l],
                mix_ssem,
                mix_rsem.at[l],
                step,
            )
            copy.start()
    lax.fori_loop(0, ie * ncol, answer, 0)

    tg_load.wait()
    targets = tg_ref[...]
    high = targets.astype(BF16)
    t_ref[0:tpd] = high
    t_ref[tpd : 2 * tpd] = (targets - high.astype(F32)).astype(BF16)
    squares = targets * targets
    lanes = 128
    folded = squares[:, 0:lanes]
    for b in range(1, squares.shape[1] // lanes):
        folded = folded + squares[:, b * lanes : (b + 1) * lanes]
    sq_high = folded.astype(BF16)
    rest = folded - sq_high.astype(F32)
    sq_mid = rest.astype(BF16)
    sq_low = (rest - sq_mid.astype(F32)).astype(BF16)
    ones = jnp.ones((8, lanes), BF16)
    row = (nt(ones, sq_high) + nt(ones, sq_mid) + nt(ones, sq_low))[0:1]
    tsq_ref[...] = jnp.zeros_like(tsq_ref)
    tsq_ref[:, 0:tpd] = row
    for step in range(1, ncol):
        col_copy(tsq_ref, tsq_in_ref.at[step - 1], tsq_ssem, tsq_rsem, step).start()

    words_load.wait()
    row_bit = jnp.left_shift(1, lax.broadcasted_iota(jnp.int32, (BITS, width), 0))

    def unpack(n):
        for w in range(nwords):
            word = words_ref[n // 2, n % 2, w : w + 1, :]
            bits = jnp.bitwise_and(jnp.broadcast_to(word, (BITS, width)), row_bit)
            signs_ref[n, w * BITS : (w + 1) * BITS, :] = jnp.where(bits != 0, 1.0, -1.0).astype(BF16)

    unpack(0)
    for n in range(2 * layers):
        if n + 1 < 2 * layers:
            unpack(n + 1)
        st = nt(signs_ref[n], g_ref[n // 2] if n % 2 == 0 else h_ref[n // 2])
        st_high = st.astype(BF16)
        st_hi_ref[n] = st_high
        st_lo_ref[n] = (st - st_high.astype(F32)).astype(BF16)
    ps_ref[...] = jnp.zeros_like(ps_ref)

    length = len_ref[0]
    position = lax.broadcasted_iota(jnp.int32, (1, seq), 1)
    weights = jnp.where(position < length, 1.0, 0.0).astype(F32) / jnp.full(
        (1, seq), length, jnp.int32
    ).astype(F32)

    def block_copy(row, block, ssem):
        return pltpu.make_async_remote_copy(
            src_ref=sk_ref.at[block],
            dst_ref=rx_ref.at[ie, ic],
            send_sem=ssem,
            recv_sem=sk_rsem.at[ie],
            device_id={"ex": row, "col": block},
            device_id_type=MESH,
        )

    def other_row(i):
        up = i + jnp.where(i >= ie, 1, 0)
        down = nex - 1 - i - jnp.where(i >= nex - 1 - ie, 1, 0)
        return jnp.where(2 * ie < nex, down, up)

    sent = 0
    for l in range(layers):
        passing(mix_in_ref.at[:, l], mix_rsem.at[l]).wait_recv()
        total = mix_ref[l]
        for step in range(1, ncol):
            total = total + mix_in_ref[step - 1, l]
        left = halves(jnp.concatenate([total[0], total[1]], axis=0) * weights)
        for j in range(2):
            n = 2 * l + j
            out = nt(left, st_hi_ref[n]) + nt(left, st_lo_ref[n])
            half = out.shape[0] // 2
            out = out[:half] + out[half:]
            at = n * m_right
            sk_ref[at // rows, at % rows : at % rows + m_right, :] = out[
                j * m_right : (j + 1) * m_right
            ]
        blocks = range(sent, 2 * (l + 1) * m_right // rows)
        sent = blocks.stop

        for block in blocks:

            @pl.when(block != ic)
            def _(block=block):
                block_copy(ie, block, own_ssem).start()

            @pl.when(block == ic)
            def _(block=block):
                pltpu.make_async_copy(
                    sk_ref.at[block], rx_ref.at[ie, ic], sk_rsem.at[ie]
                ).start()

        if l == 0:

            @pl.when(ie < nex - 1)
            def _():
                pl.semaphore_wait(ready_sem, (nex - 1 - ie) * ncol)

        def send_row(i, blocks=blocks):
            row = other_row(i)
            for block in blocks:
                block_copy(row, block, sk_ssem).start()

        repeat(nex - 1, send_row)

    tsq = tsq_ref[...]
    passing(tsq_in_ref, tsq_rsem).wait_recv()
    for step in range(1, ncol):
        tsq = tsq + tsq_in_ref[step - 1]
    t_scale = (lax.rsqrt(tsq / cols + epsilon) / math.sqrt(cols))[:, 0:tpd]

    goal = ie // groups
    slot = lax.rem(ie, groups) * ncol + ic

    def score_copy(e):
        return pltpu.make_async_remote_copy(
            src_ref=ps_ref.at[e],
            dst_ref=fin_ref.at[slot],
            send_sem=ps_ssem,
            recv_sem=fin_rsem,
            device_id={"ex": e, "col": goal},
            device_id_type=MESH,
        )

    def candidate(e):
        total = rx_ref[e, 0]
        for c in range(1, ncol):
            total = total + rx_ref[e, c]
        return total

    def stays(e):
        return jnp.logical_and(e == ie, goal == ic)

    def score(e):
        passing(rx_ref.at[e], sk_rsem.at[e]).wait_recv()
        total = candidate(e)
        part = jnp.zeros((2, 2 * tpd), F32)
        for r in range(rows):
            part = part + nt(halves(total[r : r + 1]), t_ref[:, r * k_left : (r + 1) * k_left])
        part = part[0:1] + part[1:2]
        part = (part[:, 0:tpd] + part[:, tpd : 2 * tpd]) * t_scale
        if groups > 1:
            where = lax.rem(ie, groups) * tpd
            place = (
                lax.broadcasted_iota(jnp.int32, (tpd, tpd * groups), 0) + where
                == lax.broadcasted_iota(jnp.int32, (tpd, tpd * groups), 1)
            ).astype(F32)
            part = jnp.dot(
                part, place, precision=lax.Precision.HIGHEST, preferred_element_type=F32
            )
        squares = jnp.sum(jnp.sum(total * total, axis=1, keepdims=True), axis=0, keepdims=True)
        ps_ref[e, 0:1, 0 : part.shape[1]] = part
        ps_ref[e, 1:2, :] = jnp.broadcast_to(squares, (1, 128))

        @pl.when(jnp.logical_not(stays(e)))
        def _():
            score_copy(e).start()

        @pl.when(stays(e))
        def _():
            pltpu.make_async_copy(ps_ref.at[e], fin_ref.at[slot], fin_rsem).start()

    repeat(nex, score)

    own = candidate(ie)
    passing(mix_in_ref, mix_ssem).wait_send()
    passing(tsq_in_ref, tsq_ssem).wait_send()
    passing(rx_ref.at[0, 1:ncol], own_ssem).wait_send()
    passing(rx_ref.at[1:nex], sk_ssem).wait_send()
    passing(fin_ref, fin_rsem).wait_recv()

    result = fin_ref[0, 0:1]
    for k in range(1, groups * ncol):
        result = result + fin_ref[k, 0:1]
    csq = fin_ref[0, 1:2]
    for k in range(1, ncol):
        csq = csq + fin_ref[k, 1:2]
    c_scale = lax.rsqrt(csq / cols + epsilon)
    own_scale = jnp.concatenate([c_scale] * (k_left // 128), axis=1)
    out_ref[0:rows] = own * own_scale
    out_ref[rows : rows + 1, 0:128] = result * c_scale

    @pl.when(goal == ic)
    def _():
        passing(ps_ref.at[1:nex], ps_ssem).wait_send()

    @pl.when(goal != ic)
    def _():
        passing(ps_ref, ps_ssem).wait_send()


def spread(packed_ref, feat_ref, score_ref):
    rows = packed_ref.shape[0] // 2
    k_left = packed_ref.shape[1]
    for r in range(rows):
        feat_ref[:, r * k_left : (r + 1) * k_left] = packed_ref[r : r + 1]
    score_ref[...] = packed_ref[rows : rows + 1, 0 : score_ref.shape[1]]


def on_device(
    nex,
    ncol,
    hidden_input,
    output_gradient,
    lengths,
    adapter_down,
    adapter_up,
    left_sign_words,
    right_sign_words,
    targets,
):
    examples, layers, seq, width = hidden_input.shape
    right_by_column = jnp.swapaxes(right_sign_words, 2, 3)
    nwords = left_sign_words.shape[2]
    m_right = right_sign_words.shape[3]
    k_left = nwords * BITS
    tpd, own_cols = targets.shape
    rows = own_cols // k_left
    groups = nex // ncol
    assert examples == 1 and nex == groups * ncol and rows * k_left == own_cols
    assert rows % m_right == 0 and rows * ncol == layers * 2 * m_right
    blocks = 2 * layers
    span = tpd * groups
    any_space = pl.BlockSpec(memory_space=pltpu.HBM)
    vmem = pl.BlockSpec(memory_space=pltpu.VMEM)
    peers = ncol - 1
    sems = pltpu.SemaphoreType.DMA
    packed = pl.pallas_call(
        functools.partial(kernel, nex, ncol, groups),
        out_shape=pltpu.VMEM((2 * rows, k_left), F32),
        in_specs=[any_space] * 2 + [pl.BlockSpec(memory_space=pltpu.SMEM)] + [any_space] * 5,
        out_specs=vmem,
        scratch_shapes=[
            pltpu.VMEM((layers, seq, width), BF16),
            pltpu.VMEM((layers, seq, width), BF16),
            pltpu.VMEM(adapter_down.shape, BF16),
            pltpu.VMEM(adapter_up.shape, BF16),
            pltpu.VMEM(left_sign_words.shape, jnp.int32),
            pltpu.VMEM(right_by_column.shape, jnp.int32),
            pltpu.VMEM(targets.shape, F32),
            pltpu.VMEM((blocks, k_left, width), BF16),
            pltpu.VMEM((blocks, k_left, seq), BF16),
            pltpu.VMEM((blocks, k_left, seq), BF16),
            pltpu.VMEM((2 * tpd, own_cols), BF16),
            pltpu.VMEM((blocks, 2 * m_right, width), BF16),
            pltpu.VMEM((layers, 2, m_right, seq), F32),
            pltpu.VMEM((peers, layers, 2, m_right, seq), F32),
            pltpu.VMEM((1, 128), F32),
            pltpu.VMEM((peers, 1, 128), F32),
            pltpu.VMEM((ncol, rows, k_left), F32),
            pltpu.VMEM((nex, ncol, rows, k_left), F32),
            pltpu.VMEM((nex, 2, 128), F32),
            pltpu.VMEM((groups * ncol, 2, 128), F32),
            sems((5 + 2 * layers,)),
            pltpu.SemaphoreType.REGULAR,
            sems,
            sems((layers,)),
            sems,
            sems,
            sems,
            sems,
            sems((nex,)),
            sems,
            sems,
        ],
        compiler_params=pltpu.CompilerParams(collective_id=0, has_side_effects=True),
    )(
        hidden_input,
        output_gradient,
        lengths,
        adapter_down,
        adapter_up,
        left_sign_words,
        right_by_column,
        targets,
    )
    return pl.pallas_call(
        spread,
        out_shape=(
            jax.ShapeDtypeStruct((1, own_cols), F32),
            jax.ShapeDtypeStruct((1, span), F32),
        ),
        in_specs=[vmem],
        out_specs=(vmem, vmem),
    )(pltpu.with_memory_space_constraint(packed, pltpu.VMEM))


def solution(mesh):
    return jax.shard_map(
        functools.partial(on_device, mesh.shape["ex"], mesh.shape["col"]),
        mesh=mesh,
        in_specs=(
            P(("grp", "ex"), None, None, "col"),
            P(("grp", "ex"), None, None, "col"),
            P(("grp", "ex")),
            P(None, None, "col"),
            P(None, "col", None),
            P(None, None, None, "col"),
            P(),
            P(("grp", "ex"), "col"),
        ),
        out_specs=(P(("grp", "ex"), "col"), P(("grp", "ex"), "col")),
        check_vma=False,
    )
```

```python
import functools
import math

import jax
import jax.numpy as jnp
from jax import lax
from jax.experimental import pallas as pl
from jax.experimental.pallas import tpu as pltpu
from jax.sharding import PartitionSpec as P

MESH = pl.DeviceIdType.MESH
F32 = jnp.float32
BF16 = jnp.bfloat16
BITS = 16
epsilon = 1e-06


def nt(a, b):
    return lax.dot_general(a, b, (((1,), (1,)), ((), ())), preferred_element_type=F32)


def halves(x):
    high = x.astype(BF16).astype(F32)
    return jnp.concatenate([high, x - high], axis=0).astype(BF16)


def repeat(count, body):
    if count <= 8:
        for i in range(count):
            body(i)
    else:

        def step(i, carry):
            body(i)
            return carry

        lax.fori_loop(0, count, step, 0)


def kernel(
    nex,
    ncol,
    groups,
    h_hbm,
    g_hbm,
    len_ref,
    down_hbm,
    up_hbm,
    words_hbm,
    right_hbm,
    tg_hbm,
    out_ref,
    pair_ref,
    down_ref,
    up_ref,
    words_ref,
    right_ref,
    tg_ref,
    signs_ref,
    st_out_ref,
    st_own_ref,
    st_in_ref,
    st_hi_ref,
    st_lo_ref,
    t_ref,
    fold_ref,
    mix_ref,
    mix_in_ref,
    tsq_ref,
    tsq_in_ref,
    sk_ref,
    rx_ref,
    ps_ref,
    fin_ref,
    load_sem,
    ready_sem,
    mix_ssem,
    mix_rsem,
    st_ssem,
    st_rsem,
    tsq_ssem,
    tsq_rsem,
    own_ssem,
    sk_ssem,
    sk_rsem,
    ps_ssem,
    fin_rsem,
):
    ie, ic = lax.axis_index("ex"), lax.axis_index("col")
    side, pair = lax.rem(ic, 2), ic // 2
    layers = pair_ref.shape[0]
    seq = pair_ref.shape[2]
    m_right = right_ref.shape[2]
    nwords = words_ref.shape[2]
    width = words_ref.shape[3]
    k_left = nwords * BITS
    tpd = tg_ref.shape[0]
    cols = tg_ref.shape[1] * ncol
    rows = rx_ref.shape[2]
    members = nex * ncol

    def load(n, src, dst):
        return pltpu.make_async_copy(src, dst, load_sem.at[n])

    words_load = load(0, words_hbm, words_ref)
    right_load = load(1, right_hbm, right_ref)
    down_load = load(2, down_hbm, down_ref)
    up_load = load(3, up_hbm, up_ref)
    h_loads = [load(4 + 2 * l, h_hbm.at[0, l], pair_ref.at[l, 1]) for l in range(layers)]
    g_loads = [load(5 + 2 * l, g_hbm.at[0, l], pair_ref.at[l, 0]) for l in range(layers)]
    tg_load = load(4 + 2 * layers, tg_hbm, tg_ref)
    right_load.start()
    down_load.start()
    up_load.start()
    for l in range(layers):
        h_loads[l].start()
        g_loads[l].start()
    words_load.start()
    tg_load.start()

    barrier = pltpu.get_barrier_semaphore()
    me = ie * ncol + ic

    def signal(semaphore, other):
        pl.semaphore_signal(
            semaphore,
            inc=1,
            device_id={"ex": other // ncol, "col": lax.rem(other, ncol)},
            device_id_type=MESH,
        )

    def greet(other, carry):
        @pl.when(other != me)
        def _():
            signal(barrier, other)

        return carry

    lax.fori_loop(ie * ncol, members, greet, 0)

    def answer(other, carry):
        signal(ready_sem, other)
        return carry

    def col_copy(src, dst, ssem, rsem, step):
        return pltpu.make_async_remote_copy(
            src_ref=src,
            dst_ref=dst,
            send_sem=ssem,
            recv_sem=rsem,
            device_id={"col": lax.rem(ic + step, ncol)},
            device_id_type=MESH,
        )

    def passing(buffer, semaphore):
        return pltpu.make_async_remote_copy(
            src_ref=buffer,
            dst_ref=buffer,
            send_sem=semaphore,
            recv_sem=semaphore,
            device_id={"col": ic},
            device_id_type=MESH,
        )

    right_load.wait()
    down_load.wait()
    up_load.wait()
    for l in range(layers):
        for j in range(2):
            right_t = (2 * right_ref[l, j] - 1).astype(F32).astype(BF16)
            if j == 0:
                folded = jnp.dot(right_t, down_ref[l], preferred_element_type=F32)
            else:
                folded = nt(right_t, up_ref[l])
            fold_ref[2 * l + j] = halves(folded)

    for l in range(layers):
        h_loads[l].wait()
        g_loads[l].wait()
        for j in range(2):
            both = nt(fold_ref[2 * l + j], pair_ref[l, 1 - j])
            mix_ref[l, j] = both[:m_right] + both[m_right:]
        if l == 0:
            pl.semaphore_wait(barrier, ncol - 1 + ie * ncol)
        for step in range(1, ncol):
            copy = col_copy(
                mix_ref.at[l, lax.rem(side + step, 2)],
                mix_in_ref.at[step - 1, l],
                mix_ssem,
                mix_rsem.at[l],
                step,
            )
            copy.start()
    lax.fori_loop(0, ie * ncol, answer, 0)

    tg_load.wait()
    targets = tg_ref[...]
    high = targets.astype(BF16)
    t_ref[0:tpd] = high
    t_ref[tpd : 2 * tpd] = (targets - high.astype(F32)).astype(BF16)
    squares = targets * targets
    lanes = 128
    folded = squares[:, 0:lanes]
    for b in range(1, squares.shape[1] // lanes):
        folded = folded + squares[:, b * lanes : (b + 1) * lanes]
    sq_high = folded.astype(BF16)
    rest = folded - sq_high.astype(F32)
    sq_mid = rest.astype(BF16)
    sq_low = (rest - sq_mid.astype(F32)).astype(BF16)
    ones = jnp.ones((8, lanes), BF16)
    row = (nt(ones, sq_high) + nt(ones, sq_mid) + nt(ones, sq_low))[0:1]
    tsq_ref[...] = jnp.zeros_like(tsq_ref)
    tsq_ref[:, 0:tpd] = row
    for step in range(1, ncol):
        col_copy(tsq_ref, tsq_in_ref.at[step - 1], tsq_ssem, tsq_rsem, step).start()

    words_load.wait()
    row_bit = jnp.left_shift(1, lax.broadcasted_iota(jnp.int32, (BITS, width), 0))

    def unpack(n, l, j):
        for w in range(nwords):
            word = words_ref[l, j, w : w + 1, :]
            bits = jnp.bitwise_and(jnp.broadcast_to(word, (BITS, width)), row_bit)
            signs_ref[n, w * BITS : (w + 1) * BITS, :] = jnp.where(bits != 0, 1.0, -1.0).astype(BF16)

    tasks = [(l, 1 - side) for l in range(layers)] + [(l, side) for l in range(layers)]
    st_copies = []
    unpack(0, *tasks[0])
    for n, (l, j) in enumerate(tasks):
        if n + 1 < len(tasks):
            unpack(n + 1, *tasks[n + 1])
        st = nt(signs_ref[n], pair_ref[l, j])
        if n >= layers:
            st_own_ref[l] = st
        else:
            st_out_ref[l] = st
            copy = pltpu.make_async_remote_copy(
                src_ref=st_out_ref.at[l],
                dst_ref=st_in_ref.at[l],
                send_sem=st_ssem.at[l],
                recv_sem=st_rsem.at[l],
                device_id={"col": ic + 1 - 2 * side},
                device_id_type=MESH,
            )
            copy.start()
            st_copies.append(copy)
    ps_ref[...] = jnp.zeros_like(ps_ref)

    length = len_ref[0]
    position = lax.broadcasted_iota(jnp.int32, (1, seq), 1)
    weights = jnp.where(position < length, 1.0, 0.0).astype(F32) / jnp.full(
        (1, seq), length, jnp.int32
    ).astype(F32)

    def block_copy(row, l, ssem):
        return pltpu.make_async_remote_copy(
            src_ref=sk_ref.at[l],
            dst_ref=rx_ref.at[ie, pair],
            send_sem=ssem,
            recv_sem=sk_rsem.at[ie],
            device_id={"ex": row, "col": 2 * l + side},
            device_id_type=MESH,
        )

    def other_row(i):
        up = i + jnp.where(i >= ie, 1, 0)
        down = nex - 1 - i - jnp.where(i >= nex - 1 - ie, 1, 0)
        return jnp.where(2 * ie < nex, down, up)

    for l in range(layers):
        st_copies[l].wait_recv()
        st = st_own_ref[l] + st_in_ref[l]
        st_high = st.astype(BF16)
        st_hi_ref[l] = st_high
        st_lo_ref[l] = (st - st_high.astype(F32)).astype(BF16)
    for l in range(layers):
        passing(mix_in_ref.at[:, l], mix_rsem.at[l]).wait_recv()
        total = mix_ref[l, side]
        for step in range(1, ncol):
            total = total + mix_in_ref[step - 1, l]
        left = halves(total * weights)
        out = nt(left, st_hi_ref[l]) + nt(left, st_lo_ref[l])
        sk_ref[l] = out[:m_right] + out[m_right:]

        @pl.when(pair != l)
        def _(l=l):
            block_copy(ie, l, own_ssem).start()

        @pl.when(pair == l)
        def _(l=l):
            pltpu.make_async_copy(sk_ref.at[l], rx_ref.at[ie, pair], sk_rsem.at[ie]).start()

        if l == 0:

            @pl.when(ie < nex - 1)
            def _():
                pl.semaphore_wait(ready_sem, (nex - 1 - ie) * ncol)

        def send_row(i, l=l):
            block_copy(other_row(i), l, sk_ssem).start()

        repeat(nex - 1, send_row)

    tsq = tsq_ref[...]
    passing(tsq_in_ref, tsq_rsem).wait_recv()
    for step in range(1, ncol):
        tsq = tsq + tsq_in_ref[step - 1]
    t_scale = (lax.rsqrt(tsq / cols + epsilon) / math.sqrt(cols))[:, 0:tpd]

    goal = ie // groups
    slot = lax.rem(ie, groups) * ncol + ic

    def score_copy(e):
        return pltpu.make_async_remote_copy(
            src_ref=ps_ref.at[e],
            dst_ref=fin_ref.at[slot],
            send_sem=ps_ssem,
            recv_sem=fin_rsem,
            device_id={"ex": e, "col": goal},
            device_id_type=MESH,
        )

    def candidate(e):
        total = rx_ref[e, 0]
        for p in range(1, layers):
            total = total + rx_ref[e, p]
        return total

    def stays(e):
        return jnp.logical_and(e == ie, goal == ic)

    def score(e):
        passing(rx_ref.at[e], sk_rsem.at[e]).wait_recv()
        total = candidate(e)
        part = jnp.zeros((2, 2 * tpd), F32)
        for r in range(rows):
            part = part + nt(halves(total[r : r + 1]), t_ref[:, r * k_left : (r + 1) * k_left])
        part = part[0:1] + part[1:2]
        part = (part[:, 0:tpd] + part[:, tpd : 2 * tpd]) * t_scale
        if groups > 1:
            where = lax.rem(ie, groups) * tpd
            place = (
                lax.broadcasted_iota(jnp.int32, (tpd, tpd * groups), 0) + where
                == lax.broadcasted_iota(jnp.int32, (tpd, tpd * groups), 1)
            ).astype(F32)
            part = jnp.dot(
                part, place, precision=lax.Precision.HIGHEST, preferred_element_type=F32
            )
        squares = jnp.sum(jnp.sum(total * total, axis=1, keepdims=True), axis=0, keepdims=True)
        ps_ref[e, 0:1, 0 : part.shape[1]] = part
        ps_ref[e, 1:2, :] = jnp.broadcast_to(squares, (1, 128))

        @pl.when(jnp.logical_not(stays(e)))
        def _():
            score_copy(e).start()

        @pl.when(stays(e))
        def _():
            pltpu.make_async_copy(ps_ref.at[e], fin_ref.at[slot], fin_rsem).start()

    repeat(nex, score)

    own = candidate(ie)
    passing(mix_in_ref, mix_ssem).wait_send()
    passing(tsq_in_ref, tsq_ssem).wait_send()
    for copy in st_copies:
        copy.wait_send()
    passing(rx_ref.at[0, 1:layers], own_ssem).wait_send()
    passing(rx_ref.at[1:nex], sk_ssem).wait_send()
    passing(fin_ref, fin_rsem).wait_recv()

    result = fin_ref[0, 0:1]
    for k in range(1, groups * ncol):
        result = result + fin_ref[k, 0:1]
    csq = fin_ref[0, 1:2]
    for k in range(1, ncol):
        csq = csq + fin_ref[k, 1:2]
    c_scale = lax.rsqrt(csq / cols + epsilon)
    own_scale = jnp.concatenate([c_scale] * (k_left // 128), axis=1)
    out_ref[0:rows] = own * own_scale
    out_ref[rows : rows + 1, 0:128] = result * c_scale

    @pl.when(goal == ic)
    def _():
        passing(ps_ref.at[1:nex], ps_ssem).wait_send()

    @pl.when(goal != ic)
    def _():
        passing(ps_ref, ps_ssem).wait_send()


def spread(packed_ref, feat_ref, score_ref):
    rows = packed_ref.shape[0] // 2
    k_left = packed_ref.shape[1]
    for r in range(rows):
        feat_ref[:, r * k_left : (r + 1) * k_left] = packed_ref[r : r + 1]
    score_ref[...] = packed_ref[rows : rows + 1, 0 : score_ref.shape[1]]


def on_device(
    nex,
    ncol,
    hidden_input,
    output_gradient,
    lengths,
    adapter_down,
    adapter_up,
    left_sign_words,
    right_sign_words,
    targets,
):
    examples, layers, seq, width = hidden_input.shape
    right_by_column = jnp.swapaxes(right_sign_words, 2, 3)
    nwords = left_sign_words.shape[2]
    m_right = right_sign_words.shape[3]
    k_left = nwords * BITS
    tpd, own_cols = targets.shape
    rows = own_cols // k_left
    groups = nex // ncol
    assert examples == 1 and nex == groups * ncol and rows * k_left == own_cols
    assert rows == m_right and ncol == 2 * layers
    blocks = 2 * layers
    span = tpd * groups
    any_space = pl.BlockSpec(memory_space=pltpu.HBM)
    vmem = pl.BlockSpec(memory_space=pltpu.VMEM)
    peers = ncol - 1
    sems = pltpu.SemaphoreType.DMA
    packed = pl.pallas_call(
        functools.partial(kernel, nex, ncol, groups),
        out_shape=pltpu.VMEM((2 * rows, k_left), F32),
        in_specs=[any_space] * 2 + [pl.BlockSpec(memory_space=pltpu.SMEM)] + [any_space] * 5,
        out_specs=vmem,
        scratch_shapes=[
            pltpu.VMEM((layers, 2, seq, width), BF16),
            pltpu.VMEM(adapter_down.shape, BF16),
            pltpu.VMEM(adapter_up.shape, BF16),
            pltpu.VMEM(left_sign_words.shape, jnp.int32),
            pltpu.VMEM(right_by_column.shape, jnp.int32),
            pltpu.VMEM(targets.shape, F32),
            pltpu.VMEM((blocks, k_left, width), BF16),
            pltpu.VMEM((layers, k_left, seq), F32),
            pltpu.VMEM((layers, k_left, seq), F32),
            pltpu.VMEM((layers, k_left, seq), F32),
            pltpu.VMEM((layers, k_left, seq), BF16),
            pltpu.VMEM((layers, k_left, seq), BF16),
            pltpu.VMEM((2 * tpd, own_cols), BF16),
            pltpu.VMEM((blocks, 2 * m_right, width), BF16),
            pltpu.VMEM((layers, 2, m_right, seq), F32),
            pltpu.VMEM((peers, layers, m_right, seq), F32),
            pltpu.VMEM((1, 128), F32),
            pltpu.VMEM((peers, 1, 128), F32),
            pltpu.VMEM((layers, rows, k_left), F32),
            pltpu.VMEM((nex, layers, rows, k_left), F32),
            pltpu.VMEM((nex, 2, 128), F32),
            pltpu.VMEM((groups * ncol, 2, 128), F32),
            sems((5 + 2 * layers,)),
            pltpu.SemaphoreType.REGULAR,
            sems,
            sems((layers,)),
            sems((layers,)),
            sems((layers,)),
            sems,
            sems,
            sems,
            sems,
            sems((nex,)),
            sems,
            sems,
        ],
        compiler_params=pltpu.CompilerParams(collective_id=0, has_side_effects=True),
    )(
        hidden_input,
        output_gradient,
        lengths,
        adapter_down,
        adapter_up,
        left_sign_words,
        right_by_column,
        targets,
    )
    return pl.pallas_call(
        spread,
        out_shape=(
            jax.ShapeDtypeStruct((1, own_cols), F32),
            jax.ShapeDtypeStruct((1, span), F32),
        ),
        in_specs=[vmem],
        out_specs=(vmem, vmem),
    )(pltpu.with_memory_space_constraint(packed, pltpu.VMEM))


def solution(mesh):
    return jax.shard_map(
        functools.partial(on_device, mesh.shape["ex"], mesh.shape["col"]),
        mesh=mesh,
        in_specs=(
            P(("grp", "ex"), None, None, "col"),
            P(("grp", "ex"), None, None, "col"),
            P(("grp", "ex")),
            P(None, None, "col"),
            P(None, "col", None),
            P(None, None, None, "col"),
            P(),
            P(("grp", "ex"), "col"),
        ),
        out_specs=(P(("grp", "ex"), "col"), P(("grp", "ex"), "col")),
        check_vma=False,
    )
```

```python
import functools
import math

import jax
import jax.numpy as jnp
from jax import lax
from jax.experimental import pallas as pl
from jax.experimental.pallas import tpu as pltpu
from jax.sharding import PartitionSpec as P

MESH = pl.DeviceIdType.MESH
F32 = jnp.float32
BF16 = jnp.bfloat16
BITS = 16
epsilon = 1e-06


def nt(a, b):
    return lax.dot_general(a, b, (((1,), (1,)), ((), ())), preferred_element_type=F32)


def halves(x):
    high = x.astype(BF16).astype(F32)
    return jnp.concatenate([high, x - high], axis=0).astype(BF16)


def repeat(count, body):
    if count <= 8:
        for i in range(count):
            body(i)
    else:

        def step(i, carry):
            body(i)
            return carry

        lax.fori_loop(0, count, step, 0)


def kernel(
    nex,
    ncol,
    groups,
    h_hbm,
    g_hbm,
    len_ref,
    down_hbm,
    up_hbm,
    words_hbm,
    right_hbm,
    tg_hbm,
    out_ref,
    pair_ref,
    down_ref,
    up_ref,
    words_ref,
    right_ref,
    tg_ref,
    signs_ref,
    st_out_ref,
    st_own_ref,
    st_in_ref,
    st_hi_ref,
    st_lo_ref,
    t_ref,
    fold_ref,
    mix_ref,
    mix_in_ref,
    sk_ref,
    rx_ref,
    ps_ref,
    fin_ref,
    load_sem,
    row_sem,
    ready_sem,
    mix_ssem,
    mix_rsem,
    st_ssem,
    st_rsem,
    own_ssem,
    sk_ssem,
    sk_rsem,
    ps_ssem,
    fin_rsem,
):
    ie, ic = lax.axis_index("ex"), lax.axis_index("col")
    side, pair = lax.rem(ic, 2), ic // 2
    layers = pair_ref.shape[0]
    seq = pair_ref.shape[2]
    m_right = right_ref.shape[2]
    nwords = words_ref.shape[2]
    width = words_ref.shape[3]
    k_left = nwords * BITS
    tpd = tg_ref.shape[0]
    cols = tg_ref.shape[1] * ncol
    rows = rx_ref.shape[2]
    members = nex * ncol

    def load(n, src, dst):
        return pltpu.make_async_copy(src, dst, load_sem.at[n])

    tasks = [(l, 0) for l in range(layers)] + [(l, 1) for l in range(layers)]
    words_loads = [
        load(
            4 + 2 * layers + i,
            words_hbm.at[l, side if place else 1 - side],
            words_ref.at[l, place],
        )
        for i, (l, place) in enumerate(tasks)
    ]
    right_load = load(1, right_hbm, right_ref)
    down_load = load(2, down_hbm, down_ref)
    up_load = load(3, up_hbm, up_ref)
    h_loads = [load(4 + 2 * l, h_hbm.at[0, l], pair_ref.at[l, side]) for l in range(layers)]
    g_loads = [load(5 + 2 * l, g_hbm.at[0, l], pair_ref.at[l, 1 - side]) for l in range(layers)]
    tg_load = load(0, tg_hbm, tg_ref)
    right_load.start()
    down_load.start()
    up_load.start()
    for l in range(layers):
        h_loads[l].start()
        g_loads[l].start()
    for words_load in words_loads:
        words_load.start()
    tg_load.start()

    barrier = pltpu.get_barrier_semaphore()
    me = ie * ncol + ic

    def signal(semaphore, other):
        pl.semaphore_signal(
            semaphore,
            inc=1,
            device_id={"ex": other // ncol, "col": lax.rem(other, ncol)},
            device_id_type=MESH,
        )

    first, behind = me - side, ncol - 2 * (pair + 1)

    def greet(other, carry):
        @pl.when(other != me)
        def _():
            signal(barrier, other)

        return carry

    lax.fori_loop(first, members, greet, 0)

    def answer(semaphore):
        def body(other, carry):
            signal(semaphore, other)
            return carry

        return body

    pl.semaphore_wait(barrier, first + 1)
    lax.fori_loop(ie * ncol, first, answer(row_sem), 0)
    lax.fori_loop(0, ie * ncol, answer(ready_sem), 0)

    def col_copy(src, dst, ssem, rsem, step):
        return pltpu.make_async_remote_copy(
            src_ref=src,
            dst_ref=dst,
            send_sem=ssem,
            recv_sem=rsem,
            device_id={"col": lax.rem(ic + step, ncol)},
            device_id_type=MESH,
        )

    def passing(buffer, semaphore):
        return pltpu.make_async_remote_copy(
            src_ref=buffer,
            dst_ref=buffer,
            send_sem=semaphore,
            recv_sem=semaphore,
            device_id={"col": ic},
            device_id_type=MESH,
        )

    row_bit = jnp.left_shift(1, lax.broadcasted_iota(jnp.int32, (BITS, width), 0))

    def unpack(n):
        l, place = tasks[n]
        for w in range(nwords):
            word = words_ref[l, place, w : w + 1, :]
            bits = jnp.bitwise_and(jnp.broadcast_to(word, (BITS, width)), row_bit)
            signs = jnp.where(bits != 0, 1.0, -1.0).astype(BF16)
            signs_ref[n, w * BITS : (w + 1) * BITS, :] = signs

    right_load.wait()
    down_load.wait()
    up_load.wait()
    for l in range(layers):
        for j in range(2):
            right_t = (2 * right_ref[l, j] - 1).astype(F32).astype(BF16)
            if j == 0:
                folded = jnp.dot(right_t, down_ref[l], preferred_element_type=F32)
            else:
                folded = nt(right_t, up_ref[l])
            fold_ref[2 * l + j] = halves(folded)

    for l in range(layers):
        h_loads[l].wait()
        g_loads[l].wait()
        for place in range(2):
            j = side if place else 1 - side
            both = nt(fold_ref[2 * l + j], pair_ref[l, 1 - place])
            mix_ref[l, place] = both[:m_right] + both[m_right:]
        if l == 0:


            @pl.when(behind > 0)
            def _():
                pl.semaphore_wait(row_sem, behind)

        for step in range(1, ncol):
            copy = col_copy(
                mix_ref.at[l, 1 - step % 2],
                mix_in_ref.at[step - 1, l],
                mix_ssem,
                mix_rsem.at[l],
                step,
            )
            copy.start()

    for words_load in words_loads:
        words_load.wait()
    unpack(0)
    def st_copy(l):
        return pltpu.make_async_remote_copy(
            src_ref=st_out_ref.at[l],
            dst_ref=st_in_ref.at[l],
            send_sem=st_ssem.at[l],
            recv_sem=st_rsem.at[l],
            device_id={"col": ic + 1 - 2 * side},
            device_id_type=MESH,
        )

    def join(l):
        st_copy(l).wait_recv()
        st = st_own_ref[l] + st_in_ref[l]
        st_high = st.astype(BF16)
        st_hi_ref[l] = st_high
        st_lo_ref[l] = (st - st_high.astype(F32)).astype(BF16)

    for n, (l, place) in enumerate(tasks):
        if n + 1 < len(tasks):
            unpack(n + 1)
        st = nt(signs_ref[n], pair_ref[l, place])
        if n >= layers:
            st_own_ref[l] = st
        else:
            st_out_ref[l] = st
        if n == layers - 1:
            for m in range(layers):
                st_copy(m).start()
    for l in range(layers - 1):
        join(l)
    join(layers - 1)
    ps_ref[...] = jnp.zeros_like(ps_ref)

    length = len_ref[0]
    position = lax.broadcasted_iota(jnp.int32, (1, seq), 1)
    weights = jnp.where(position < length, 1.0, 0.0).astype(F32) / jnp.full(
        (1, seq), length, jnp.int32
    ).astype(F32)

    def block_copy(row, l, ssem):
        return pltpu.make_async_remote_copy(
            src_ref=sk_ref.at[l],
            dst_ref=rx_ref.at[ie, pair],
            send_sem=ssem,
            recv_sem=sk_rsem.at[ie],
            device_id={"ex": row, "col": 2 * l + side},
            device_id_type=MESH,
        )

    def other_row(i):
        up = i + jnp.where(i >= ie, 1, 0)
        down = nex - 1 - i - jnp.where(i >= nex - 1 - ie, 1, 0)
        return jnp.where(2 * ie < nex, down, up)

    for l in range(layers):
        passing(mix_in_ref.at[:, l], mix_rsem.at[l]).wait_recv()
        total = mix_ref[l, 1]
        for step in range(1, ncol):
            total = total + mix_in_ref[step - 1, l]
        left = halves(total * weights)
        out = nt(left, st_hi_ref[l]) + nt(left, st_lo_ref[l])
        sk_ref[l] = out[:m_right] + out[m_right:]

        @pl.when(pair != l)
        def _(l=l):
            block_copy(ie, l, own_ssem).start()

        @pl.when(pair == l)
        def _(l=l):
            pltpu.make_async_copy(sk_ref.at[l], rx_ref.at[ie, pair], sk_rsem.at[ie]).start()

        if l == 0:

            @pl.when(ie < nex - 1)
            def _():
                pl.semaphore_wait(ready_sem, (nex - 1 - ie) * ncol)

        def send_row(i, l=l):
            block_copy(other_row(i), l, sk_ssem).start()

        repeat(nex - 1, send_row)

    tg_load.wait()
    targets = tg_ref[...]
    high = targets.astype(BF16)
    t_ref[0:tpd] = high
    t_ref[tpd : 2 * tpd] = (targets - high.astype(F32)).astype(BF16)
    squares = targets * targets
    lanes = 128
    folded = squares[:, 0:lanes]
    for b in range(1, squares.shape[1] // lanes):
        folded = folded + squares[:, b * lanes : (b + 1) * lanes]
    sq_high = folded.astype(BF16)
    rest = folded - sq_high.astype(F32)
    sq_mid = rest.astype(BF16)
    sq_low = (rest - sq_mid.astype(F32)).astype(BF16)
    ones = jnp.ones((8, lanes), BF16)
    tsq = (nt(ones, sq_high) + nt(ones, sq_mid) + nt(ones, sq_low))[0:1]

    def placed(values):
        if groups == 1:
            return values
        where = lax.rem(ie, groups) * tpd
        place = (
            lax.broadcasted_iota(jnp.int32, (tpd, tpd * groups), 0) + where
            == lax.broadcasted_iota(jnp.int32, (tpd, tpd * groups), 1)
        ).astype(F32)
        return jnp.dot(values, place, precision=lax.Precision.HIGHEST, preferred_element_type=F32)

    tsq = placed(tsq)
    span = tsq.shape[1]
    for e in range(nex):
        ps_ref[e, 2:3, 0:span] = tsq

    goal = ie // groups
    slot = lax.rem(ie, groups) * ncol + ic

    def score_copy(e):
        return pltpu.make_async_remote_copy(
            src_ref=ps_ref.at[e],
            dst_ref=fin_ref.at[slot],
            send_sem=ps_ssem,
            recv_sem=fin_rsem,
            device_id={"ex": e, "col": goal},
            device_id_type=MESH,
        )

    def candidate(e):
        total = rx_ref[e, 0]
        for p in range(1, layers):
            total = total + rx_ref[e, p]
        return total

    def stays(e):
        return jnp.logical_and(e == ie, goal == ic)

    def score(e):
        passing(rx_ref.at[e], sk_rsem.at[e]).wait_recv()
        total = candidate(e)
        part = jnp.zeros((2, 2 * tpd), F32)
        for r in range(rows):
            part = part + nt(halves(total[r : r + 1]), t_ref[:, r * k_left : (r + 1) * k_left])
        part = part[0:1] + part[1:2]
        part = placed(part[:, 0:tpd] + part[:, tpd : 2 * tpd])
        squares = jnp.sum(jnp.sum(total * total, axis=1, keepdims=True), axis=0, keepdims=True)
        ps_ref[e, 0:1, 0:span] = part
        ps_ref[e, 1:2, :] = jnp.broadcast_to(squares, (1, 128))

        @pl.when(jnp.logical_not(stays(e)))
        def _():
            score_copy(e).start()

        @pl.when(stays(e))
        def _():
            pltpu.make_async_copy(ps_ref.at[e], fin_ref.at[slot], fin_rsem).start()

    repeat(nex, score)

    own = candidate(ie)
    passing(mix_in_ref, mix_ssem).wait_send()
    for l in range(layers):
        st_copy(l).wait_send()
    passing(rx_ref.at[0, 1:layers], own_ssem).wait_send()
    passing(rx_ref.at[1:nex], sk_ssem).wait_send()
    passing(fin_ref, fin_rsem).wait_recv()

    sums = fin_ref[0]
    for k in range(1, groups * ncol):
        sums = sums + fin_ref[k]
    csq = fin_ref[0, 1:2]
    for k in range(1, ncol):
        csq = csq + fin_ref[k, 1:2]
    t_scale = lax.rsqrt(sums[2:3] / cols + epsilon) / math.sqrt(cols)
    c_scale = lax.rsqrt(csq / cols + epsilon)
    own_scale = jnp.concatenate([c_scale] * (k_left // 128), axis=1)
    out_ref[0:rows] = own * own_scale
    out_ref[rows : rows + 1, 0:128] = sums[0:1] * t_scale * c_scale

    @pl.when(goal == ic)
    def _():
        passing(ps_ref.at[1:nex], ps_ssem).wait_send()

    @pl.when(goal != ic)
    def _():
        passing(ps_ref, ps_ssem).wait_send()


def spread(packed_ref, feat_ref, score_ref):
    rows = packed_ref.shape[0] // 2
    k_left = packed_ref.shape[1]
    for r in range(rows):
        feat_ref[:, r * k_left : (r + 1) * k_left] = packed_ref[r : r + 1]
    score_ref[...] = packed_ref[rows : rows + 1, 0 : score_ref.shape[1]]


def on_device(
    nex,
    ncol,
    hidden_input,
    output_gradient,
    lengths,
    adapter_down,
    adapter_up,
    left_sign_words,
    right_sign_words,
    targets,
):
    examples, layers, seq, width = hidden_input.shape
    right_by_column = jnp.swapaxes(right_sign_words, 2, 3)
    nwords = left_sign_words.shape[2]
    m_right = right_sign_words.shape[3]
    k_left = nwords * BITS
    tpd, own_cols = targets.shape
    rows = own_cols // k_left
    groups = nex // ncol
    assert examples == 1 and nex == groups * ncol and rows * k_left == own_cols
    assert rows == m_right and ncol == 2 * layers
    blocks = 2 * layers
    span = tpd * groups
    any_space = pl.BlockSpec(memory_space=pltpu.HBM)
    vmem = pl.BlockSpec(memory_space=pltpu.VMEM)
    peers = ncol - 1
    sems = pltpu.SemaphoreType.DMA
    packed = pl.pallas_call(
        functools.partial(kernel, nex, ncol, groups),
        out_shape=pltpu.VMEM((2 * rows, k_left), F32),
        in_specs=[any_space] * 2 + [pl.BlockSpec(memory_space=pltpu.SMEM)] + [any_space] * 5,
        out_specs=vmem,
        scratch_shapes=[
            pltpu.VMEM((layers, 2, seq, width), BF16),
            pltpu.VMEM(adapter_down.shape, BF16),
            pltpu.VMEM(adapter_up.shape, BF16),
            pltpu.VMEM(left_sign_words.shape, jnp.int32),
            pltpu.VMEM(right_by_column.shape, jnp.int32),
            pltpu.VMEM(targets.shape, F32),
            pltpu.VMEM((blocks, k_left, width), BF16),
            pltpu.VMEM((layers, k_left, seq), F32),
            pltpu.VMEM((layers, k_left, seq), F32),
            pltpu.VMEM((layers, k_left, seq), F32),
            pltpu.VMEM((layers, k_left, seq), BF16),
            pltpu.VMEM((layers, k_left, seq), BF16),
            pltpu.VMEM((2 * tpd, own_cols), BF16),
            pltpu.VMEM((blocks, 2 * m_right, width), BF16),
            pltpu.VMEM((layers, 2, m_right, seq), F32),
            pltpu.VMEM((peers, layers, m_right, seq), F32),
            pltpu.VMEM((layers, rows, k_left), F32),
            pltpu.VMEM((nex, layers, rows, k_left), F32),
            pltpu.VMEM((nex, 4, 128), F32),
            pltpu.VMEM((groups * ncol, 4, 128), F32),
            sems((4 + 2 * layers + blocks,)),
            pltpu.SemaphoreType.REGULAR,
            pltpu.SemaphoreType.REGULAR,
            sems,
            sems((layers,)),
            sems((layers,)),
            sems((layers,)),
            sems,
            sems,
            sems((nex,)),
            sems,
            sems,
        ],
        compiler_params=pltpu.CompilerParams(collective_id=0, has_side_effects=True),
    )(
        hidden_input,
        output_gradient,
        lengths,
        adapter_down,
        adapter_up,
        left_sign_words,
        right_by_column,
        targets,
    )
    return pl.pallas_call(
        spread,
        out_shape=(
            jax.ShapeDtypeStruct((1, own_cols), F32),
            jax.ShapeDtypeStruct((1, span), F32),
        ),
        in_specs=[vmem],
        out_specs=(vmem, vmem),
    )(pltpu.with_memory_space_constraint(packed, pltpu.VMEM))


def solution(mesh):
    return jax.shard_map(
        functools.partial(on_device, mesh.shape["ex"], mesh.shape["col"]),
        mesh=mesh,
        in_specs=(
            P(("grp", "ex"), None, None, "col"),
            P(("grp", "ex"), None, None, "col"),
            P(("grp", "ex")),
            P(None, None, "col"),
            P(None, "col", None),
            P(None, None, None, "col"),
            P(),
            P(("grp", "ex"), "col"),
        ),
        out_specs=(P(("grp", "ex"), "col"), P(("grp", "ex"), "col")),
        check_vma=False,
    )
```

```python
import functools
import math

import jax
import jax.numpy as jnp
from jax import lax
from jax.experimental import pallas as pl
from jax.experimental.pallas import tpu as pltpu
from jax.sharding import PartitionSpec as P

MESH = pl.DeviceIdType.MESH
F32 = jnp.float32
BF16 = jnp.bfloat16
BITS = 16
epsilon = 1e-06


def nt(a, b):
    return lax.dot_general(a, b, (((1,), (1,)), ((), ())), preferred_element_type=F32)


def halves(x):
    high = x.astype(BF16).astype(F32)
    return jnp.concatenate([high, x - high], axis=0).astype(BF16)


def repeat(count, body):
    if count <= 8:
        for i in range(count):
            body(i)
    else:

        def step(i, carry):
            body(i)
            return carry

        lax.fori_loop(0, count, step, 0)


def kernel(
    nex,
    ncol,
    groups,
    h_hbm,
    g_hbm,
    len_ref,
    down_hbm,
    up_hbm,
    words_hbm,
    right_hbm,
    tg_hbm,
    out_ref,
    pair_ref,
    down_ref,
    up_ref,
    words_ref,
    right_ref,
    tg_ref,
    signs_ref,
    st_out_ref,
    st_own_ref,
    st_in_ref,
    st_hi_ref,
    st_lo_ref,
    t_ref,
    fold_ref,
    mix_ref,
    mix_in_ref,
    sk_ref,
    rx_ref,
    ps_ref,
    fin_ref,
    load_sem,
    row_sem,
    ready_sem,
    mix_ssem,
    mix_rsem,
    st_ssem,
    st_rsem,
    own_ssem,
    sk_ssem,
    sk_rsem,
    ps_ssem,
    fin_rsem,
):
    ie, ic = lax.axis_index("ex"), lax.axis_index("col")
    side, pair = lax.rem(ic, 2), ic // 2
    layers = pair_ref.shape[0]
    seq = pair_ref.shape[2]
    m_right = right_ref.shape[2]
    nwords = words_ref.shape[2]
    width = words_ref.shape[3]
    k_left = nwords * BITS
    tpd = tg_ref.shape[0]
    cols = tg_ref.shape[1] * ncol
    rows = rx_ref.shape[2]
    members = nex * ncol

    def load(n, src, dst):
        return pltpu.make_async_copy(src, dst, load_sem.at[n])

    tasks = [(l, 0) for l in range(layers)] + [(l, 1) for l in range(layers)]
    words_loads = [
        load(
            4 + 2 * layers + i,
            words_hbm.at[l, side if place else 1 - side],
            words_ref.at[l, place],
        )
        for i, (l, place) in enumerate(tasks)
    ]
    right_load = load(1, right_hbm, right_ref)
    down_load = load(2, down_hbm, down_ref)
    up_load = load(3, up_hbm, up_ref)
    h_loads = [load(4 + 2 * l, h_hbm.at[0, l], pair_ref.at[l, side]) for l in range(layers)]
    g_loads = [load(5 + 2 * l, g_hbm.at[0, l], pair_ref.at[l, 1 - side]) for l in range(layers)]
    tg_load = load(0, tg_hbm, tg_ref)
    right_load.start()
    down_load.start()
    up_load.start()
    for l in range(layers):
        h_loads[l].start()
        g_loads[l].start()
    for words_load in words_loads:
        words_load.start()
    tg_load.start()

    barrier = pltpu.get_barrier_semaphore()
    me = ie * ncol + ic

    def signal(semaphore, other):
        pl.semaphore_signal(
            semaphore,
            inc=1,
            device_id={"ex": other // ncol, "col": lax.rem(other, ncol)},
            device_id_type=MESH,
        )

    first, behind = me - side, ncol - 2 * (pair + 1)

    def greet(other, carry):
        @pl.when(other != me)
        def _():
            signal(barrier, other)

        return carry

    lax.fori_loop(first, members, greet, 0)

    def answer(semaphore):
        def body(other, carry):
            signal(semaphore, other)
            return carry

        return body

    pl.semaphore_wait(barrier, first + 1)
    lax.fori_loop(ie * ncol, first, answer(row_sem), 0)
    lax.fori_loop(0, ie * ncol, answer(ready_sem), 0)

    def col_copy(src, dst, ssem, rsem, step):
        return pltpu.make_async_remote_copy(
            src_ref=src,
            dst_ref=dst,
            send_sem=ssem,
            recv_sem=rsem,
            device_id={"col": lax.rem(ic + step, ncol)},
            device_id_type=MESH,
        )

    def passing(buffer, semaphore):
        return pltpu.make_async_remote_copy(
            src_ref=buffer,
            dst_ref=buffer,
            send_sem=semaphore,
            recv_sem=semaphore,
            device_id={"col": ic},
            device_id_type=MESH,
        )

    row_bit = jnp.left_shift(1, lax.broadcasted_iota(jnp.int32, (BITS, width), 0)).astype(jnp.int16)

    def unpack(n):
        l, place = tasks[n]
        for w in range(nwords):
            word = words_ref[l, place, w : w + 1, :]
            bits = jnp.bitwise_and(jnp.broadcast_to(word, (BITS, width)).astype(jnp.int16), row_bit)
            signs = jnp.where(bits != 0, jnp.bfloat16(1.0), jnp.bfloat16(-1.0))
            signs_ref[n, w * BITS : (w + 1) * BITS, :] = signs

    right_load.wait()
    down_load.wait()
    up_load.wait()
    for l in range(layers):
        for j in range(2):
            right_t = (2 * right_ref[l, j] - 1).astype(F32).astype(BF16)
            if j == 0:
                folded = jnp.dot(right_t, down_ref[l], preferred_element_type=F32)
            else:
                folded = nt(right_t, up_ref[l])
            fold_ref[2 * l + j] = halves(folded)

    for l in range(layers):
        h_loads[l].wait()
        g_loads[l].wait()
        for place in range(2):
            j = side if place else 1 - side
            both = nt(fold_ref[2 * l + j], pair_ref[l, 1 - place])
            mix_ref[l, place] = both[:m_right] + both[m_right:]
        if l == 0:


            @pl.when(behind > 0)
            def _():
                pl.semaphore_wait(row_sem, behind)

        for step in range(1, ncol):
            copy = col_copy(
                mix_ref.at[l, 1 - step % 2],
                mix_in_ref.at[step - 1, l],
                mix_ssem,
                mix_rsem.at[l],
                step,
            )
            copy.start()

    for words_load in words_loads:
        words_load.wait()
    unpack(0)
    def st_copy(l):
        return pltpu.make_async_remote_copy(
            src_ref=st_out_ref.at[l],
            dst_ref=st_in_ref.at[l],
            send_sem=st_ssem.at[l],
            recv_sem=st_rsem.at[l],
            device_id={"col": ic + 1 - 2 * side},
            device_id_type=MESH,
        )

    def join(l):
        st_copy(l).wait_recv()
        st = st_own_ref[l] + st_in_ref[l]
        st_high = st.astype(BF16)
        st_hi_ref[l] = st_high
        st_lo_ref[l] = (st - st_high.astype(F32)).astype(BF16)

    for n, (l, place) in enumerate(tasks):
        if n + 1 < len(tasks):
            unpack(n + 1)
        st = nt(signs_ref[n], pair_ref[l, place])
        if n >= layers:
            st_own_ref[l] = st
        else:
            st_out_ref[l] = st
        if n == layers - 1:
            for m in range(layers):
                st_copy(m).start()
    ps_ref[...] = jnp.zeros_like(ps_ref)

    length = len_ref[0]
    position = lax.broadcasted_iota(jnp.int32, (1, seq), 1)
    weights = jnp.where(position < length, 1.0, 0.0).astype(F32) / jnp.full(
        (1, seq), length, jnp.int32
    ).astype(F32)

    def block_copy(row, l, ssem):
        return pltpu.make_async_remote_copy(
            src_ref=sk_ref.at[l],
            dst_ref=rx_ref.at[ie, pair],
            send_sem=ssem,
            recv_sem=sk_rsem.at[ie],
            device_id={"ex": row, "col": 2 * l + side},
            device_id_type=MESH,
        )

    def other_row(i):
        up = i + jnp.where(i >= ie, 1, 0)
        down = nex - 1 - i - jnp.where(i >= nex - 1 - ie, 1, 0)
        return jnp.where(2 * ie < nex, down, up)

    for l in range(layers):
        join(l)
        passing(mix_in_ref.at[:, l], mix_rsem.at[l]).wait_recv()
        total = mix_ref[l, 1]
        for step in range(1, ncol):
            total = total + mix_in_ref[step - 1, l]
        left = halves(total * weights)
        out = nt(left, st_hi_ref[l]) + nt(left, st_lo_ref[l])
        sk_ref[l] = out[:m_right] + out[m_right:]

        @pl.when(pair != l)
        def _(l=l):
            block_copy(ie, l, own_ssem).start()

        @pl.when(pair == l)
        def _(l=l):
            pltpu.make_async_copy(sk_ref.at[l], rx_ref.at[ie, pair], sk_rsem.at[ie]).start()

        if l == 0:

            @pl.when(ie < nex - 1)
            def _():
                pl.semaphore_wait(ready_sem, (nex - 1 - ie) * ncol)

        def send_row(i, l=l):
            block_copy(other_row(i), l, sk_ssem).start()

        repeat(nex - 1, send_row)

    tg_load.wait()
    targets = tg_ref[...]
    high = targets.astype(BF16)
    t_ref[0:tpd] = high
    t_ref[tpd : 2 * tpd] = (targets - high.astype(F32)).astype(BF16)
    squares = targets * targets
    lanes = 128
    folded = squares[:, 0:lanes]
    for b in range(1, squares.shape[1] // lanes):
        folded = folded + squares[:, b * lanes : (b + 1) * lanes]
    sq_high = folded.astype(BF16)
    rest = folded - sq_high.astype(F32)
    sq_mid = rest.astype(BF16)
    sq_low = (rest - sq_mid.astype(F32)).astype(BF16)
    ones = jnp.ones((8, lanes), BF16)
    tsq = (nt(ones, sq_high) + nt(ones, sq_mid) + nt(ones, sq_low))[0:1]

    def placed(values):
        if groups == 1:
            return values
        where = lax.rem(ie, groups) * tpd
        place = (
            lax.broadcasted_iota(jnp.int32, (tpd, tpd * groups), 0) + where
            == lax.broadcasted_iota(jnp.int32, (tpd, tpd * groups), 1)
        ).astype(F32)
        return jnp.dot(values, place, precision=lax.Precision.HIGHEST, preferred_element_type=F32)

    tsq = placed(tsq)
    span = tsq.shape[1]
    for e in range(nex):
        ps_ref[e, 2:3, 0:span] = tsq

    goal = ie // groups
    slot = lax.rem(ie, groups) * ncol + ic

    def score_copy(e):
        return pltpu.make_async_remote_copy(
            src_ref=ps_ref.at[e],
            dst_ref=fin_ref.at[slot],
            send_sem=ps_ssem,
            recv_sem=fin_rsem,
            device_id={"ex": e, "col": goal},
            device_id_type=MESH,
        )

    def candidate(e):
        total = rx_ref[e, 0]
        for p in range(1, layers):
            total = total + rx_ref[e, p]
        return total

    def stays(e):
        return jnp.logical_and(e == ie, goal == ic)

    def score(e):
        passing(rx_ref.at[e], sk_rsem.at[e]).wait_recv()
        total = candidate(e)
        part = jnp.zeros((2, 2 * tpd), F32)
        for r in range(rows):
            part = part + nt(halves(total[r : r + 1]), t_ref[:, r * k_left : (r + 1) * k_left])
        part = part[0:1] + part[1:2]
        part = placed(part[:, 0:tpd] + part[:, tpd : 2 * tpd])
        squares = jnp.sum(jnp.sum(total * total, axis=1, keepdims=True), axis=0, keepdims=True)
        ps_ref[e, 0:1, 0:span] = part
        ps_ref[e, 1:2, :] = jnp.broadcast_to(squares, (1, 128))

        @pl.when(jnp.logical_not(stays(e)))
        def _():
            score_copy(e).start()

        @pl.when(stays(e))
        def _():
            pltpu.make_async_copy(ps_ref.at[e], fin_ref.at[slot], fin_rsem).start()

    repeat(nex, score)

    own = candidate(ie)
    passing(mix_in_ref, mix_ssem).wait_send()
    for l in range(layers):
        st_copy(l).wait_send()
    passing(rx_ref.at[0, 1:layers], own_ssem).wait_send()
    passing(rx_ref.at[1:nex], sk_ssem).wait_send()
    passing(fin_ref, fin_rsem).wait_recv()

    sums = fin_ref[0]
    for k in range(1, groups * ncol):
        sums = sums + fin_ref[k]
    csq = fin_ref[0, 1:2]
    for k in range(1, ncol):
        csq = csq + fin_ref[k, 1:2]
    t_scale = lax.rsqrt(sums[2:3] / cols + epsilon) / math.sqrt(cols)
    c_scale = lax.rsqrt(csq / cols + epsilon)
    own_scale = jnp.concatenate([c_scale] * (k_left // 128), axis=1)
    out_ref[0:rows] = own * own_scale
    out_ref[rows : rows + 1, 0:128] = sums[0:1] * t_scale * c_scale

    @pl.when(goal == ic)
    def _():
        passing(ps_ref.at[1:nex], ps_ssem).wait_send()

    @pl.when(goal != ic)
    def _():
        passing(ps_ref, ps_ssem).wait_send()


def spread(packed_ref, feat_ref, score_ref):
    rows = packed_ref.shape[0] // 2
    k_left = packed_ref.shape[1]
    for r in range(rows):
        feat_ref[:, r * k_left : (r + 1) * k_left] = packed_ref[r : r + 1]
    score_ref[...] = packed_ref[rows : rows + 1, 0 : score_ref.shape[1]]


def on_device(
    nex,
    ncol,
    hidden_input,
    output_gradient,
    lengths,
    adapter_down,
    adapter_up,
    left_sign_words,
    right_sign_words,
    targets,
):
    examples, layers, seq, width = hidden_input.shape
    right_by_column = jnp.swapaxes(right_sign_words, 2, 3)
    nwords = left_sign_words.shape[2]
    m_right = right_sign_words.shape[3]
    k_left = nwords * BITS
    tpd, own_cols = targets.shape
    rows = own_cols // k_left
    groups = nex // ncol
    assert examples == 1 and nex == groups * ncol and rows * k_left == own_cols
    assert rows == m_right and ncol == 2 * layers
    blocks = 2 * layers
    span = tpd * groups
    any_space = pl.BlockSpec(memory_space=pltpu.HBM)
    vmem = pl.BlockSpec(memory_space=pltpu.VMEM)
    peers = ncol - 1
    sems = pltpu.SemaphoreType.DMA
    packed = pl.pallas_call(
        functools.partial(kernel, nex, ncol, groups),
        out_shape=pltpu.VMEM((2 * rows, k_left), F32),
        in_specs=[any_space] * 2 + [pl.BlockSpec(memory_space=pltpu.SMEM)] + [any_space] * 5,
        out_specs=vmem,
        scratch_shapes=[
            pltpu.VMEM((layers, 2, seq, width), BF16),
            pltpu.VMEM(adapter_down.shape, BF16),
            pltpu.VMEM(adapter_up.shape, BF16),
            pltpu.VMEM(left_sign_words.shape, jnp.int32),
            pltpu.VMEM(right_by_column.shape, jnp.int32),
            pltpu.VMEM(targets.shape, F32),
            pltpu.VMEM((blocks, k_left, width), BF16),
            pltpu.VMEM((layers, k_left, seq), F32),
            pltpu.VMEM((layers, k_left, seq), F32),
            pltpu.VMEM((layers, k_left, seq), F32),
            pltpu.VMEM((layers, k_left, seq), BF16),
            pltpu.VMEM((layers, k_left, seq), BF16),
            pltpu.VMEM((2 * tpd, own_cols), BF16),
            pltpu.VMEM((blocks, 2 * m_right, width), BF16),
            pltpu.VMEM((layers, 2, m_right, seq), F32),
            pltpu.VMEM((peers, layers, m_right, seq), F32),
            pltpu.VMEM((layers, rows, k_left), F32),
            pltpu.VMEM((nex, layers, rows, k_left), F32),
            pltpu.VMEM((nex, 4, 128), F32),
            pltpu.VMEM((groups * ncol, 4, 128), F32),
            sems((4 + 2 * layers + blocks,)),
            pltpu.SemaphoreType.REGULAR,
            pltpu.SemaphoreType.REGULAR,
            sems,
            sems((layers,)),
            sems((layers,)),
            sems((layers,)),
            sems,
            sems,
            sems((nex,)),
            sems,
            sems,
        ],
        compiler_params=pltpu.CompilerParams(collective_id=0, has_side_effects=True),
    )(
        hidden_input,
        output_gradient,
        lengths,
        adapter_down,
        adapter_up,
        left_sign_words,
        right_by_column,
        targets,
    )
    return pl.pallas_call(
        spread,
        out_shape=(
            jax.ShapeDtypeStruct((1, own_cols), F32),
            jax.ShapeDtypeStruct((1, span), F32),
        ),
        in_specs=[vmem],
        out_specs=(vmem, vmem),
    )(pltpu.with_memory_space_constraint(packed, pltpu.VMEM))


def solution(mesh):
    return jax.shard_map(
        functools.partial(on_device, mesh.shape["ex"], mesh.shape["col"]),
        mesh=mesh,
        in_specs=(
            P(("grp", "ex"), None, None, "col"),
            P(("grp", "ex"), None, None, "col"),
            P(("grp", "ex")),
            P(None, None, "col"),
            P(None, "col", None),
            P(None, None, None, "col"),
            P(),
            P(("grp", "ex"), "col"),
        ),
        out_specs=(P(("grp", "ex"), "col"), P(("grp", "ex"), "col")),
        check_vma=False,
    )
```

```python
import functools
import math

import jax
import jax.numpy as jnp
from jax import lax
from jax.experimental import pallas as pl
from jax.experimental.pallas import tpu as pltpu
from jax.sharding import PartitionSpec as P

MESH = pl.DeviceIdType.MESH
F32 = jnp.float32
BF16 = jnp.bfloat16
BITS = 16
epsilon = 1e-06


def nt(a, b):
    return lax.dot_general(a, b, (((1,), (1,)), ((), ())), preferred_element_type=F32)


def halves(x):
    high = x.astype(BF16).astype(F32)
    return jnp.concatenate([high, x - high], axis=0).astype(BF16)


def repeat(count, body):
    if count <= 8:
        for i in range(count):
            body(i)
    else:

        def step(i, carry):
            body(i)
            return carry

        lax.fori_loop(0, count, step, 0)


def kernel(
    nex,
    ncol,
    groups,
    h_hbm,
    g_hbm,
    len_ref,
    down_hbm,
    up_hbm,
    words_hbm,
    right_hbm,
    tg_hbm,
    out_ref,
    pair_ref,
    down_ref,
    up_ref,
    words_ref,
    right_ref,
    tg_ref,
    signs_ref,
    st_out_ref,
    st_own_ref,
    st_in_ref,
    st_hi_ref,
    st_lo_ref,
    t_ref,
    fold_ref,
    mix_ref,
    mix_in_ref,
    sk_ref,
    rx_ref,
    ps_ref,
    fin_ref,
    load_sem,
    row_sem,
    ready_sem,
    mix_ssem,
    mix_rsem,
    st_ssem,
    st_rsem,
    own_ssem,
    sk_ssem,
    sk_rsem,
    ps_ssem,
    fin_rsem,
):
    ie, ic = lax.axis_index("ex"), lax.axis_index("col")
    side, pair = lax.rem(ic, 2), ic // 2
    layers = pair_ref.shape[0]
    seq = pair_ref.shape[2]
    m_right = right_ref.shape[2]
    nwords = words_ref.shape[2]
    width = words_ref.shape[3]
    k_left = nwords * BITS
    tpd = tg_ref.shape[0]
    cols = tg_ref.shape[1] * ncol
    rows = rx_ref.shape[2]
    members = nex * ncol

    def load(n, src, dst):
        return pltpu.make_async_copy(src, dst, load_sem.at[n])

    tasks = [(l, 0) for l in range(layers)] + [(l, 1) for l in range(layers)]
    words_loads = [
        load(
            4 + 2 * layers,
            words_hbm.at[l, side if place else 1 - side],
            words_ref.at[l, place],
        )
        for l, place in tasks
    ]
    right_load = load(1, right_hbm, right_ref)
    down_load = load(2, down_hbm, down_ref)
    up_load = load(3, up_hbm, up_ref)
    h_loads = [load(4 + 2 * l, h_hbm.at[0, l], pair_ref.at[l, side]) for l in range(layers)]
    g_loads = [load(5 + 2 * l, g_hbm.at[0, l], pair_ref.at[l, 1 - side]) for l in range(layers)]
    tg_load = load(0, tg_hbm, tg_ref)
    right_load.start()
    down_load.start()
    up_load.start()
    for l in range(layers):
        h_loads[l].start()
        g_loads[l].start()
    for words_load in words_loads:
        words_load.start()
    tg_load.start()

    barrier = pltpu.get_barrier_semaphore()
    me = ie * ncol + ic

    def signal(semaphore, other):
        pl.semaphore_signal(
            semaphore,
            inc=1,
            device_id={"ex": other // ncol, "col": lax.rem(other, ncol)},
            device_id_type=MESH,
        )

    first, behind = me - side, ncol - 2 * (pair + 1)

    def greet(other, carry):
        @pl.when(other != me)
        def _():
            signal(barrier, other)

        return carry

    lax.fori_loop(first, members, greet, 0)

    def answer(semaphore):
        def body(other, carry):
            signal(semaphore, other)
            return carry

        return body

    pl.semaphore_wait(barrier, first + 1)
    lax.fori_loop(ie * ncol, first, answer(row_sem), 0)
    lax.fori_loop(0, ie * ncol, answer(ready_sem), 0)

    def col_copy(src, dst, ssem, rsem, step):
        return pltpu.make_async_remote_copy(
            src_ref=src,
            dst_ref=dst,
            send_sem=ssem,
            recv_sem=rsem,
            device_id={"col": lax.rem(ic + step, ncol)},
            device_id_type=MESH,
        )

    def passing(buffer, semaphore):
        return pltpu.make_async_remote_copy(
            src_ref=buffer,
            dst_ref=buffer,
            send_sem=semaphore,
            recv_sem=semaphore,
            device_id={"col": ic},
            device_id_type=MESH,
        )

    row_bit = jnp.left_shift(1, lax.broadcasted_iota(jnp.int32, (BITS, width), 0)).astype(jnp.int16)

    def unpack(n):
        l, place = tasks[n]
        for w in range(nwords):
            word = words_ref[l, place, w : w + 1, :]
            bits = jnp.bitwise_and(jnp.broadcast_to(word, (BITS, width)).astype(jnp.int16), row_bit)
            signs = jnp.where(bits != 0, jnp.bfloat16(1.0), jnp.bfloat16(-1.0))
            signs_ref[n, w * BITS : (w + 1) * BITS, :] = signs

    right_load.wait()
    down_load.wait()
    up_load.wait()
    for l in range(layers):
        for j in range(2):
            right_t = (2 * right_ref[l, j] - 1).astype(F32).astype(BF16)
            if j == 0:
                folded = jnp.dot(right_t, down_ref[l], preferred_element_type=F32)
            else:
                folded = nt(right_t, up_ref[l])
            fold_ref[2 * l + j] = halves(folded)

    for l in range(layers):
        h_loads[l].wait()
        g_loads[l].wait()
        for place in range(2):
            j = side if place else 1 - side
            both = nt(fold_ref[2 * l + j], pair_ref[l, 1 - place])
            mix_ref[l, place] = both[:m_right] + both[m_right:]
        if l == 0:


            @pl.when(behind > 0)
            def _():
                pl.semaphore_wait(row_sem, behind)

        for step in range(1, ncol):
            copy = col_copy(
                mix_ref.at[l, 1 - step % 2],
                mix_in_ref.at[step - 1, l],
                mix_ssem,
                mix_rsem.at[l],
                step,
            )
            copy.start()

    load(4 + 2 * layers, words_ref, words_ref).wait()
    unpack(0)
    def st_copy(l):
        return pltpu.make_async_remote_copy(
            src_ref=st_out_ref.at[l],
            dst_ref=st_in_ref.at[l],
            send_sem=st_ssem.at[l],
            recv_sem=st_rsem.at[l],
            device_id={"col": ic + 1 - 2 * side},
            device_id_type=MESH,
        )

    def join(l):
        st_copy(l).wait_recv()
        st = st_own_ref[l] + st_in_ref[l]
        st_high = st.astype(BF16)
        st_hi_ref[l] = st_high
        st_lo_ref[l] = (st - st_high.astype(F32)).astype(BF16)

    for n, (l, place) in enumerate(tasks):
        if n + 1 < len(tasks):
            unpack(n + 1)
        st = nt(signs_ref[n], pair_ref[l, place])
        if n >= layers:
            st_own_ref[l] = st
        else:
            st_out_ref[l] = st
        if n == layers - 1:
            for m in range(layers):
                st_copy(m).start()
    ps_ref[...] = jnp.zeros_like(ps_ref)

    length = len_ref[0]
    position = lax.broadcasted_iota(jnp.int32, (1, seq), 1)
    weights = jnp.where(position < length, 1.0, 0.0).astype(F32) / jnp.full(
        (1, seq), length, jnp.int32
    ).astype(F32)

    def block_copy(row, l, ssem):
        return pltpu.make_async_remote_copy(
            src_ref=sk_ref.at[l],
            dst_ref=rx_ref.at[ie, pair],
            send_sem=ssem,
            recv_sem=sk_rsem.at[ie],
            device_id={"ex": row, "col": 2 * l + side},
            device_id_type=MESH,
        )

    def other_row(i):
        up = i + jnp.where(i >= ie, 1, 0)
        down = nex - 1 - i - jnp.where(i >= nex - 1 - ie, 1, 0)
        return jnp.where(2 * ie < nex, down, up)

    for l in range(layers):
        join(l)
        passing(mix_in_ref.at[:, l], mix_rsem.at[l]).wait_recv()
        total = mix_ref[l, 1]
        for step in range(1, ncol):
            total = total + mix_in_ref[step - 1, l]
        left = halves(total * weights)
        out = nt(left, st_hi_ref[l]) + nt(left, st_lo_ref[l])
        sk_ref[l] = out[:m_right] + out[m_right:]

        @pl.when(pair != l)
        def _(l=l):
            block_copy(ie, l, own_ssem).start()

        @pl.when(pair == l)
        def _(l=l):
            pltpu.make_async_copy(sk_ref.at[l], rx_ref.at[ie, pair], sk_rsem.at[ie]).start()

        if l == 0:

            @pl.when(ie < nex - 1)
            def _():
                pl.semaphore_wait(ready_sem, (nex - 1 - ie) * ncol)

        def send_row(i, l=l):
            block_copy(other_row(i), l, sk_ssem).start()

        repeat(nex - 1, send_row)

    tg_load.wait()
    targets = tg_ref[...]
    high = targets.astype(BF16)
    t_ref[0:tpd] = high
    t_ref[tpd : 2 * tpd] = (targets - high.astype(F32)).astype(BF16)
    squares = targets * targets
    lanes = 128
    folded = squares[:, 0:lanes]
    for b in range(1, squares.shape[1] // lanes):
        folded = folded + squares[:, b * lanes : (b + 1) * lanes]
    sq_high = folded.astype(BF16)
    rest = folded - sq_high.astype(F32)
    sq_mid = rest.astype(BF16)
    sq_low = (rest - sq_mid.astype(F32)).astype(BF16)
    ones = jnp.ones((8, lanes), BF16)
    tsq = (nt(ones, sq_high) + nt(ones, sq_mid) + nt(ones, sq_low))[0:1]

    def placed(values):
        if groups == 1:
            return values
        where = lax.rem(ie, groups) * tpd
        place = (
            lax.broadcasted_iota(jnp.int32, (tpd, tpd * groups), 0) + where
            == lax.broadcasted_iota(jnp.int32, (tpd, tpd * groups), 1)
        ).astype(F32)
        return jnp.dot(values, place, precision=lax.Precision.HIGHEST, preferred_element_type=F32)

    tsq = placed(tsq)
    span = tsq.shape[1]
    for e in range(nex):
        ps_ref[e, 2:3, 0:span] = tsq

    goal = ie // groups
    slot = lax.rem(ie, groups) * ncol + ic

    def score_copy(e):
        return pltpu.make_async_remote_copy(
            src_ref=ps_ref.at[e],
            dst_ref=fin_ref.at[slot],
            send_sem=ps_ssem,
            recv_sem=fin_rsem,
            device_id={"ex": e, "col": goal},
            device_id_type=MESH,
        )

    def candidate(e):
        total = rx_ref[e, 0]
        for p in range(1, layers):
            total = total + rx_ref[e, p]
        return total

    def stays(e):
        return jnp.logical_and(e == ie, goal == ic)

    def score(e):
        passing(rx_ref.at[e], sk_rsem.at[e]).wait_recv()
        total = candidate(e)
        feats = jnp.concatenate([total[r : r + 1] for r in range(rows)], axis=1)
        part = nt(halves(feats), t_ref[...])
        part = part[0:1] + part[1:2]
        part = placed(part[:, 0:tpd] + part[:, tpd : 2 * tpd])
        squares = jnp.sum(jnp.sum(total * total, axis=1, keepdims=True), axis=0, keepdims=True)
        ps_ref[e, 0:1, 0:span] = part
        ps_ref[e, 1:2, :] = jnp.broadcast_to(squares, (1, 128))

        @pl.when(jnp.logical_not(stays(e)))
        def _():
            score_copy(e).start()

        @pl.when(stays(e))
        def _():
            pltpu.make_async_copy(ps_ref.at[e], fin_ref.at[slot], fin_rsem).start()

    repeat(nex, score)

    own = candidate(ie)
    passing(mix_in_ref, mix_ssem).wait_send()
    for l in range(layers):
        st_copy(l).wait_send()
    passing(rx_ref.at[0, 1:layers], own_ssem).wait_send()
    passing(rx_ref.at[1:nex], sk_ssem).wait_send()
    passing(fin_ref, fin_rsem).wait_recv()

    sums = fin_ref[0]
    for k in range(1, groups * ncol):
        sums = sums + fin_ref[k]
    csq = fin_ref[0, 1:2]
    for k in range(1, ncol):
        csq = csq + fin_ref[k, 1:2]
    t_scale = lax.rsqrt(sums[2:3] / cols + epsilon) / math.sqrt(cols)
    c_scale = lax.rsqrt(csq / cols + epsilon)
    own_scale = jnp.concatenate([c_scale] * (k_left // 128), axis=1)
    out_ref[0:rows] = own * own_scale
    out_ref[rows : rows + 1, 0:128] = sums[0:1] * t_scale * c_scale

    @pl.when(goal == ic)
    def _():
        passing(ps_ref.at[1:nex], ps_ssem).wait_send()

    @pl.when(goal != ic)
    def _():
        passing(ps_ref, ps_ssem).wait_send()


def spread(packed_ref, feat_ref, score_ref):
    rows = packed_ref.shape[0] // 2
    k_left = packed_ref.shape[1]
    for r in range(rows):
        feat_ref[:, r * k_left : (r + 1) * k_left] = packed_ref[r : r + 1]
    score_ref[...] = packed_ref[rows : rows + 1, 0 : score_ref.shape[1]]


def on_device(
    nex,
    ncol,
    hidden_input,
    output_gradient,
    lengths,
    adapter_down,
    adapter_up,
    left_sign_words,
    right_sign_words,
    targets,
):
    examples, layers, seq, width = hidden_input.shape
    right_by_column = jnp.swapaxes(right_sign_words, 2, 3)
    nwords = left_sign_words.shape[2]
    m_right = right_sign_words.shape[3]
    k_left = nwords * BITS
    tpd, own_cols = targets.shape
    rows = own_cols // k_left
    groups = nex // ncol
    assert examples == 1 and nex == groups * ncol and rows * k_left == own_cols
    assert rows == m_right and ncol == 2 * layers
    blocks = 2 * layers
    span = tpd * groups
    any_space = pl.BlockSpec(memory_space=pltpu.HBM)
    vmem = pl.BlockSpec(memory_space=pltpu.VMEM)
    peers = ncol - 1
    sems = pltpu.SemaphoreType.DMA
    packed = pl.pallas_call(
        functools.partial(kernel, nex, ncol, groups),
        out_shape=pltpu.VMEM((2 * rows, k_left), F32),
        in_specs=[any_space] * 2 + [pl.BlockSpec(memory_space=pltpu.SMEM)] + [any_space] * 5,
        out_specs=vmem,
        scratch_shapes=[
            pltpu.VMEM((layers, 2, seq, width), BF16),
            pltpu.VMEM(adapter_down.shape, BF16),
            pltpu.VMEM(adapter_up.shape, BF16),
            pltpu.VMEM(left_sign_words.shape, jnp.int32),
            pltpu.VMEM(right_by_column.shape, jnp.int32),
            pltpu.VMEM(targets.shape, F32),
            pltpu.VMEM((blocks, k_left, width), BF16),
            pltpu.VMEM((layers, k_left, seq), F32),
            pltpu.VMEM((layers, k_left, seq), F32),
            pltpu.VMEM((layers, k_left, seq), F32),
            pltpu.VMEM((layers, k_left, seq), BF16),
            pltpu.VMEM((layers, k_left, seq), BF16),
            pltpu.VMEM((2 * tpd, own_cols), BF16),
            pltpu.VMEM((blocks, 2 * m_right, width), BF16),
            pltpu.VMEM((layers, 2, m_right, seq), F32),
            pltpu.VMEM((peers, layers, m_right, seq), F32),
            pltpu.VMEM((layers, rows, k_left), F32),
            pltpu.VMEM((nex, layers, rows, k_left), F32),
            pltpu.VMEM((nex, 4, 128), F32),
            pltpu.VMEM((groups * ncol, 4, 128), F32),
            sems((5 + 2 * layers,)),
            pltpu.SemaphoreType.REGULAR,
            pltpu.SemaphoreType.REGULAR,
            sems,
            sems((layers,)),
            sems((layers,)),
            sems((layers,)),
            sems,
            sems,
            sems((nex,)),
            sems,
            sems,
        ],
        compiler_params=pltpu.CompilerParams(collective_id=0, has_side_effects=True),
    )(
        hidden_input,
        output_gradient,
        lengths,
        adapter_down,
        adapter_up,
        left_sign_words,
        right_by_column,
        targets,
    )
    return pl.pallas_call(
        spread,
        out_shape=(
            jax.ShapeDtypeStruct((1, own_cols), F32),
            jax.ShapeDtypeStruct((1, span), F32),
        ),
        in_specs=[vmem],
        out_specs=(vmem, vmem),
    )(pltpu.with_memory_space_constraint(packed, pltpu.VMEM))


def solution(mesh):
    return jax.shard_map(
        functools.partial(on_device, mesh.shape["ex"], mesh.shape["col"]),
        mesh=mesh,
        in_specs=(
            P(("grp", "ex"), None, None, "col"),
            P(("grp", "ex"), None, None, "col"),
            P(("grp", "ex")),
            P(None, None, "col"),
            P(None, "col", None),
            P(None, None, None, "col"),
            P(),
            P(("grp", "ex"), "col"),
        ),
        out_specs=(P(("grp", "ex"), "col"), P(("grp", "ex"), "col")),
        check_vma=False,
    )
```

```python
import functools
import math

import jax
import jax.numpy as jnp
from jax import lax
from jax.experimental import pallas as pl
from jax.experimental.pallas import tpu as pltpu
from jax.sharding import PartitionSpec as P

MESH = pl.DeviceIdType.MESH
F32 = jnp.float32
BF16 = jnp.bfloat16
BITS = 16
epsilon = 1e-06


def nt(a, b):
    return lax.dot_general(a, b, (((1,), (1,)), ((), ())), preferred_element_type=F32)


def halves(x):
    high = x.astype(BF16).astype(F32)
    return jnp.concatenate([high, x - high], axis=0).astype(BF16)


def repeat(count, body):
    if count <= 8:
        for i in range(count):
            body(i)
    else:

        def step(i, carry):
            body(i)
            return carry

        lax.fori_loop(0, count, step, 0)


def kernel(
    nex,
    ncol,
    groups,
    h_hbm,
    g_hbm,
    len_ref,
    down_hbm,
    up_hbm,
    words_hbm,
    right_hbm,
    tg_hbm,
    out_ref,
    pair_ref,
    down_ref,
    up_ref,
    words_ref,
    right_ref,
    tg_ref,
    signs_ref,
    st_out_ref,
    st_own_ref,
    st_in_ref,
    st_hi_ref,
    st_lo_ref,
    t_ref,
    fold_ref,
    mix_ref,
    mix_in_ref,
    sk_ref,
    rx_ref,
    ps_ref,
    fin_ref,
    load_sem,
    row_sem,
    ready_sem,
    mix_ssem,
    mix_rsem,
    st_ssem,
    st_rsem,
    own_ssem,
    sk_ssem,
    sk_rsem,
    ps_ssem,
    fin_rsem,
):
    ie, ic = lax.axis_index("ex"), lax.axis_index("col")
    side, pair = lax.rem(ic, 2), ic // 2
    layers = pair_ref.shape[0]
    seq = pair_ref.shape[2]
    m_right = right_ref.shape[2]
    nwords = words_ref.shape[2]
    width = words_ref.shape[3]
    k_left = nwords * BITS
    tpd = tg_ref.shape[0]
    cols = tg_ref.shape[1] * ncol
    rows = rx_ref.shape[2]
    members = nex * ncol

    def load(n, src, dst):
        return pltpu.make_async_copy(src, dst, load_sem.at[n])

    tasks = [(l, 0) for l in range(layers)] + [(l, 1) for l in range(layers)]
    words_loads = [
        load(
            4 + 2 * layers,
            words_hbm.at[l, side if place else 1 - side],
            words_ref.at[l, place],
        )
        for l, place in tasks
    ]
    right_load = load(1, right_hbm, right_ref)
    down_load = load(2, down_hbm, down_ref)
    up_load = load(3, up_hbm, up_ref)
    h_loads = [load(4 + 2 * l, h_hbm.at[0, l], pair_ref.at[l, side]) for l in range(layers)]
    g_loads = [load(5 + 2 * l, g_hbm.at[0, l], pair_ref.at[l, 1 - side]) for l in range(layers)]
    tg_load = load(0, tg_hbm, tg_ref)
    right_load.start()
    down_load.start()
    up_load.start()
    for l in range(layers):
        h_loads[l].start()
        g_loads[l].start()
    for words_load in words_loads:
        words_load.start()
    tg_load.start()

    barrier = pltpu.get_barrier_semaphore()
    me = ie * ncol + ic

    def signal(semaphore, other):
        pl.semaphore_signal(
            semaphore,
            inc=1,
            device_id={"ex": other // ncol, "col": lax.rem(other, ncol)},
            device_id_type=MESH,
        )

    first, behind = me - side, ncol - 2 * (pair + 1)

    def greet(other, carry):
        @pl.when(other != me)
        def _():
            signal(barrier, other)

        return carry

    lax.fori_loop(first, members, greet, 0)

    def answer(semaphore):
        def body(other, carry):
            signal(semaphore, other)
            return carry

        return body

    pl.semaphore_wait(barrier, first + 1)
    lax.fori_loop(ie * ncol, first, answer(row_sem), 0)
    lax.fori_loop(0, ie * ncol, answer(ready_sem), 0)

    def col_copy(src, dst, ssem, rsem, step):
        return pltpu.make_async_remote_copy(
            src_ref=src,
            dst_ref=dst,
            send_sem=ssem,
            recv_sem=rsem,
            device_id={"col": lax.rem(ic + step, ncol)},
            device_id_type=MESH,
        )

    def passing(buffer, semaphore):
        return pltpu.make_async_remote_copy(
            src_ref=buffer,
            dst_ref=buffer,
            send_sem=semaphore,
            recv_sem=semaphore,
            device_id={"col": ic},
            device_id_type=MESH,
        )

    row_bit = jnp.left_shift(1, lax.broadcasted_iota(jnp.int32, (BITS, width), 0)).astype(jnp.int16)

    def unpack(n):
        l, place = tasks[n]
        for w in range(nwords):
            word = words_ref[l, place, w : w + 1, :]
            bits = jnp.bitwise_and(jnp.broadcast_to(word, (BITS, width)).astype(jnp.int16), row_bit)
            signs = jnp.where(bits != 0, jnp.bfloat16(1.0), jnp.bfloat16(-1.0))
            signs_ref[n, w * BITS : (w + 1) * BITS, :] = signs

    right_load.wait()
    down_load.wait()
    up_load.wait()
    for l in range(layers):
        for j in range(2):
            right_t = (2 * right_ref[l, j] - 1).astype(F32).astype(BF16)
            if j == 0:
                folded = jnp.dot(right_t, down_ref[l], preferred_element_type=F32)
            else:
                folded = nt(right_t, up_ref[l])
            fold_ref[2 * l + j] = halves(folded)

    for l in range(layers):
        h_loads[l].wait()
        g_loads[l].wait()
        for place in range(2):
            j = side if place else 1 - side
            both = nt(fold_ref[2 * l + j], pair_ref[l, 1 - place])
            mix_ref[l, place] = both[:m_right] + both[m_right:]
        if l == 0:


            @pl.when(behind > 0)
            def _():
                pl.semaphore_wait(row_sem, behind)

        for step in range(1, ncol):
            copy = col_copy(
                mix_ref.at[l, 1 - step % 2],
                mix_in_ref.at[step - 1, l],
                mix_ssem,
                mix_rsem.at[l],
                step,
            )
            copy.start()

    load(4 + 2 * layers, words_ref, words_ref).wait()
    unpack(0)
    def st_copy(l):
        return pltpu.make_async_remote_copy(
            src_ref=st_out_ref.at[l],
            dst_ref=st_in_ref.at[l],
            send_sem=st_ssem.at[l],
            recv_sem=st_rsem.at[l],
            device_id={"col": ic + 1 - 2 * side},
            device_id_type=MESH,
        )

    def join(l):
        st_copy(l).wait_recv()
        st = st_own_ref[l] + st_in_ref[l]
        st_high = st.astype(BF16)
        st_hi_ref[l] = st_high
        st_lo_ref[l] = (st - st_high.astype(F32)).astype(BF16)

    for n, (l, place) in enumerate(tasks):
        if n + 1 < len(tasks):
            unpack(n + 1)
        st = nt(signs_ref[n], pair_ref[l, place])
        if n >= layers:
            st_own_ref[l] = st
        else:
            st_out_ref[l] = st
        if n == layers - 1:
            for m in range(layers):
                st_copy(m).start()
    ps_ref[...] = jnp.zeros_like(ps_ref)

    length = len_ref[0]
    position = lax.broadcasted_iota(jnp.int32, (1, seq), 1)
    weights = jnp.where(position < length, 1.0, 0.0).astype(F32) / jnp.full(
        (1, seq), length, jnp.int32
    ).astype(F32)

    def block_copy(row, l, ssem):
        return pltpu.make_async_remote_copy(
            src_ref=sk_ref.at[l],
            dst_ref=rx_ref.at[ie, pair],
            send_sem=ssem,
            recv_sem=sk_rsem.at[ie],
            device_id={"ex": row, "col": 2 * l + side},
            device_id_type=MESH,
        )

    def other_row(i):
        up = i + jnp.where(i >= ie, 1, 0)
        down = nex - 1 - i - jnp.where(i >= nex - 1 - ie, 1, 0)
        return jnp.where(2 * ie < nex, down, up)

    for l in range(layers):
        passing(mix_in_ref.at[:, l], mix_rsem.at[l]).wait_recv()
        total = mix_ref[l, 1]
        for step in range(1, ncol):
            total = total + mix_in_ref[step - 1, l]
        left = halves(total * weights)
        join(l)
        out = nt(left, st_hi_ref[l]) + nt(left, st_lo_ref[l])
        sk_ref[l] = out[:m_right] + out[m_right:]

        @pl.when(pair != l)
        def _(l=l):
            block_copy(ie, l, own_ssem).start()

        @pl.when(pair == l)
        def _(l=l):
            pltpu.make_async_copy(sk_ref.at[l], rx_ref.at[ie, pair], sk_rsem.at[ie]).start()

        if l == 0:

            @pl.when(ie < nex - 1)
            def _():
                pl.semaphore_wait(ready_sem, (nex - 1 - ie) * ncol)

        def send_row(i, l=l):
            block_copy(other_row(i), l, sk_ssem).start()

        repeat(nex - 1, send_row)

    tg_load.wait()
    targets = tg_ref[...]
    high = targets.astype(BF16)
    t_ref[0:tpd] = high
    t_ref[tpd : 2 * tpd] = (targets - high.astype(F32)).astype(BF16)
    squares = targets * targets
    lanes = 128
    folded = squares[:, 0:lanes]
    for b in range(1, squares.shape[1] // lanes):
        folded = folded + squares[:, b * lanes : (b + 1) * lanes]
    sq_high = folded.astype(BF16)
    rest = folded - sq_high.astype(F32)
    sq_mid = rest.astype(BF16)
    sq_low = (rest - sq_mid.astype(F32)).astype(BF16)
    ones = jnp.ones((8, lanes), BF16)
    tsq = (nt(ones, sq_high) + nt(ones, sq_mid) + nt(ones, sq_low))[0:1]

    def placed(values):
        if groups == 1:
            return values
        where = lax.rem(ie, groups) * tpd
        place = (
            lax.broadcasted_iota(jnp.int32, (tpd, tpd * groups), 0) + where
            == lax.broadcasted_iota(jnp.int32, (tpd, tpd * groups), 1)
        ).astype(F32)
        return jnp.dot(values, place, precision=lax.Precision.HIGHEST, preferred_element_type=F32)

    tsq = placed(tsq)
    span = tsq.shape[1]
    for e in range(nex):
        ps_ref[e, 2:3, 0:span] = tsq

    goal = ie // groups
    slot = lax.rem(ie, groups) * ncol + ic

    def score_copy(e):
        return pltpu.make_async_remote_copy(
            src_ref=ps_ref.at[e],
            dst_ref=fin_ref.at[slot],
            send_sem=ps_ssem,
            recv_sem=fin_rsem,
            device_id={"ex": e, "col": goal},
            device_id_type=MESH,
        )

    def candidate(e):
        total = rx_ref[e, 0]
        for p in range(1, layers):
            total = total + rx_ref[e, p]
        return total

    def stays(e):
        return jnp.logical_and(e == ie, goal == ic)

    def score(e):
        passing(rx_ref.at[e], sk_rsem.at[e]).wait_recv()
        total = candidate(e)
        feats = jnp.concatenate([total[r : r + 1] for r in range(rows)], axis=1)
        part = nt(halves(feats), t_ref[...])
        part = part[0:1] + part[1:2]
        part = placed(part[:, 0:tpd] + part[:, tpd : 2 * tpd])
        squares = jnp.sum(jnp.sum(total * total, axis=1, keepdims=True), axis=0, keepdims=True)
        ps_ref[e, 0:1, 0:span] = part
        ps_ref[e, 1:2, :] = jnp.broadcast_to(squares, (1, 128))

        @pl.when(jnp.logical_not(stays(e)))
        def _():
            score_copy(e).start()

        @pl.when(stays(e))
        def _():
            pltpu.make_async_copy(ps_ref.at[e], fin_ref.at[slot], fin_rsem).start()

    repeat(nex, score)

    own = candidate(ie)
    passing(mix_in_ref, mix_ssem).wait_send()
    for l in range(layers):
        st_copy(l).wait_send()
    passing(rx_ref.at[0, 1:layers], own_ssem).wait_send()
    passing(rx_ref.at[1:nex], sk_ssem).wait_send()
    passing(fin_ref, fin_rsem).wait_recv()

    sums = fin_ref[0]
    for k in range(1, groups * ncol):
        sums = sums + fin_ref[k]
    csq = fin_ref[0, 1:2]
    for k in range(1, ncol):
        csq = csq + fin_ref[k, 1:2]
    t_scale = lax.rsqrt(sums[2:3] / cols + epsilon) / math.sqrt(cols)
    c_scale = lax.rsqrt(csq / cols + epsilon)
    own_scale = jnp.concatenate([c_scale] * (k_left // 128), axis=1)
    out_ref[0:rows] = own * own_scale
    out_ref[rows : rows + 1, 0:128] = sums[0:1] * t_scale * c_scale

    @pl.when(goal == ic)
    def _():
        passing(ps_ref.at[1:nex], ps_ssem).wait_send()

    @pl.when(goal != ic)
    def _():
        passing(ps_ref, ps_ssem).wait_send()


def spread(packed_ref, feat_ref, score_ref):
    rows = packed_ref.shape[0] // 2
    k_left = packed_ref.shape[1]
    for r in range(rows):
        feat_ref[:, r * k_left : (r + 1) * k_left] = packed_ref[r : r + 1]
    score_ref[...] = packed_ref[rows : rows + 1, 0 : score_ref.shape[1]]


def on_device(
    nex,
    ncol,
    hidden_input,
    output_gradient,
    lengths,
    adapter_down,
    adapter_up,
    left_sign_words,
    right_sign_words,
    targets,
):
    examples, layers, seq, width = hidden_input.shape
    right_by_column = jnp.swapaxes(right_sign_words, 2, 3)
    nwords = left_sign_words.shape[2]
    m_right = right_sign_words.shape[3]
    k_left = nwords * BITS
    tpd, own_cols = targets.shape
    rows = own_cols // k_left
    groups = nex // ncol
    assert examples == 1 and nex == groups * ncol and rows * k_left == own_cols
    assert rows == m_right and ncol == 2 * layers
    blocks = 2 * layers
    span = tpd * groups
    any_space = pl.BlockSpec(memory_space=pltpu.HBM)
    vmem = pl.BlockSpec(memory_space=pltpu.VMEM)
    peers = ncol - 1
    sems = pltpu.SemaphoreType.DMA
    packed = pl.pallas_call(
        functools.partial(kernel, nex, ncol, groups),
        out_shape=pltpu.VMEM((2 * rows, k_left), F32),
        in_specs=[any_space] * 2 + [pl.BlockSpec(memory_space=pltpu.SMEM)] + [any_space] * 5,
        out_specs=vmem,
        scratch_shapes=[
            pltpu.VMEM((layers, 2, seq, width), BF16),
            pltpu.VMEM(adapter_down.shape, BF16),
            pltpu.VMEM(adapter_up.shape, BF16),
            pltpu.VMEM(left_sign_words.shape, jnp.int32),
            pltpu.VMEM(right_by_column.shape, jnp.int32),
            pltpu.VMEM(targets.shape, F32),
            pltpu.VMEM((blocks, k_left, width), BF16),
            pltpu.VMEM((layers, k_left, seq), F32),
            pltpu.VMEM((layers, k_left, seq), F32),
            pltpu.VMEM((layers, k_left, seq), F32),
            pltpu.VMEM((layers, k_left, seq), BF16),
            pltpu.VMEM((layers, k_left, seq), BF16),
            pltpu.VMEM((2 * tpd, own_cols), BF16),
            pltpu.VMEM((blocks, 2 * m_right, width), BF16),
            pltpu.VMEM((layers, 2, m_right, seq), F32),
            pltpu.VMEM((peers, layers, m_right, seq), F32),
            pltpu.VMEM((layers, rows, k_left), F32),
            pltpu.VMEM((nex, layers, rows, k_left), F32),
            pltpu.VMEM((nex, 4, 128), F32),
            pltpu.VMEM((groups * ncol, 4, 128), F32),
            sems((5 + 2 * layers,)),
            pltpu.SemaphoreType.REGULAR,
            pltpu.SemaphoreType.REGULAR,
            sems,
            sems((layers,)),
            sems((layers,)),
            sems((layers,)),
            sems,
            sems,
            sems((nex,)),
            sems,
            sems,
        ],
        compiler_params=pltpu.CompilerParams(collective_id=0, has_side_effects=True),
    )(
        hidden_input,
        output_gradient,
        lengths,
        adapter_down,
        adapter_up,
        left_sign_words,
        right_by_column,
        targets,
    )
    return pl.pallas_call(
        spread,
        out_shape=(
            jax.ShapeDtypeStruct((1, own_cols), F32),
            jax.ShapeDtypeStruct((1, span), F32),
        ),
        in_specs=[vmem],
        out_specs=(vmem, vmem),
    )(pltpu.with_memory_space_constraint(packed, pltpu.VMEM))


def solution(mesh):
    return jax.shard_map(
        functools.partial(on_device, mesh.shape["ex"], mesh.shape["col"]),
        mesh=mesh,
        in_specs=(
            P(("grp", "ex"), None, None, "col"),
            P(("grp", "ex"), None, None, "col"),
            P(("grp", "ex")),
            P(None, None, "col"),
            P(None, "col", None),
            P(None, None, None, "col"),
            P(),
            P(("grp", "ex"), "col"),
        ),
        out_specs=(P(("grp", "ex"), "col"), P(("grp", "ex"), "col")),
        check_vma=False,
    )
```

```python
import functools
import math

import jax
import jax.numpy as jnp
from jax import lax
from jax.experimental import pallas as pl
from jax.experimental.pallas import tpu as pltpu
from jax.sharding import PartitionSpec as P

MESH = pl.DeviceIdType.MESH
F32 = jnp.float32
BF16 = jnp.bfloat16
BITS = 16
epsilon = 1e-06


def nt(a, b):
    return lax.dot_general(a, b, (((1,), (1,)), ((), ())), preferred_element_type=F32)


def halves(x):
    high = x.astype(BF16).astype(F32)
    return jnp.concatenate([high, x - high], axis=0).astype(BF16)


def repeat(count, body):
    if count <= 8:
        for i in range(count):
            body(i)
    else:

        def step(i, carry):
            body(i)
            return carry

        lax.fori_loop(0, count, step, 0)


def kernel(
    nex,
    ncol,
    groups,
    h_hbm,
    g_hbm,
    len_ref,
    down_hbm,
    up_hbm,
    words_hbm,
    right_hbm,
    tg_hbm,
    out_ref,
    pair_ref,
    down_ref,
    up_ref,
    words_ref,
    right_ref,
    tg_ref,
    signs_ref,
    st_out_ref,
    st_own_ref,
    st_in_ref,
    st_hi_ref,
    st_lo_ref,
    t_ref,
    fold_ref,
    mix_ref,
    mix_in_ref,
    sk_ref,
    rx_ref,
    ps_ref,
    fin_ref,
    load_sem,
    row_sem,
    ready_sem,
    mix_ssem,
    mix_rsem,
    st_ssem,
    st_rsem,
    own_ssem,
    sk_ssem,
    sk_rsem,
    ps_ssem,
    fin_rsem,
):
    ie, ic = lax.axis_index("ex"), lax.axis_index("col")
    side, pair = lax.rem(ic, 2), ic // 2
    layers = pair_ref.shape[0]
    seq = pair_ref.shape[2]
    m_right = right_ref.shape[2]
    nwords = words_ref.shape[2]
    width = words_ref.shape[3]
    k_left = nwords * BITS
    tpd = tg_ref.shape[0]
    cols = tg_ref.shape[1] * ncol
    rows = rx_ref.shape[2]
    members = nex * ncol

    def load(n, src, dst):
        return pltpu.make_async_copy(src, dst, load_sem.at[n])

    tasks = [(l, 0) for l in range(layers)] + [(l, 1) for l in range(layers)]
    words_loads = [
        load(
            4 + 2 * layers,
            words_hbm.at[l, side if place else 1 - side],
            words_ref.at[l, place],
        )
        for l, place in tasks
    ]
    right_load = load(1, right_hbm, right_ref)
    down_load = load(2, down_hbm, down_ref)
    up_load = load(3, up_hbm, up_ref)
    h_loads = [load(4 + 2 * l, h_hbm.at[0, l], pair_ref.at[l, side]) for l in range(layers)]
    g_loads = [load(5 + 2 * l, g_hbm.at[0, l], pair_ref.at[l, 1 - side]) for l in range(layers)]
    tg_load = load(0, tg_hbm, tg_ref)
    right_load.start()
    down_load.start()
    up_load.start()
    for l in range(layers):
        h_loads[l].start()
        g_loads[l].start()
    for words_load in words_loads:
        words_load.start()
    tg_load.start()

    barrier = pltpu.get_barrier_semaphore()
    me = ie * ncol + ic

    def signal(semaphore, other):
        pl.semaphore_signal(
            semaphore,
            inc=1,
            device_id={"ex": other // ncol, "col": lax.rem(other, ncol)},
            device_id_type=MESH,
        )

    first, behind = me - side, ncol - 2 * (pair + 1)

    def greet(other, carry):
        @pl.when(other != me)
        def _():
            signal(barrier, other)

        return carry

    lax.fori_loop(first, members, greet, 0)

    def answer(semaphore):
        def body(other, carry):
            signal(semaphore, other)
            return carry

        return body

    pl.semaphore_wait(barrier, first + 1)
    lax.fori_loop(ie * ncol, first, answer(row_sem), 0)
    lax.fori_loop(0, ie * ncol, answer(ready_sem), 0)

    def col_copy(src, dst, ssem, rsem, step):
        return pltpu.make_async_remote_copy(
            src_ref=src,
            dst_ref=dst,
            send_sem=ssem,
            recv_sem=rsem,
            device_id={"col": lax.rem(ic + step, ncol)},
            device_id_type=MESH,
        )

    def passing(buffer, semaphore):
        return pltpu.make_async_remote_copy(
            src_ref=buffer,
            dst_ref=buffer,
            send_sem=semaphore,
            recv_sem=semaphore,
            device_id={"col": ic},
            device_id_type=MESH,
        )

    row_bit = jnp.left_shift(1, lax.broadcasted_iota(jnp.int32, (BITS, width), 0)).astype(jnp.int16)

    def unpack(n):
        l, place = tasks[n]
        for w in range(nwords):
            word = words_ref[l, place, w : w + 1, :]
            bits = jnp.bitwise_and(jnp.broadcast_to(word, (BITS, width)).astype(jnp.int16), row_bit)
            signs = jnp.where(bits != 0, jnp.bfloat16(1.0), jnp.bfloat16(-1.0))
            signs_ref[n, w * BITS : (w + 1) * BITS, :] = signs

    right_load.wait()
    down_load.wait()
    up_load.wait()
    for l in range(layers):
        for j in range(2):
            right_t = (2 * right_ref[l, j] - 1).astype(F32).astype(BF16)
            if j == 0:
                folded = jnp.dot(right_t, down_ref[l], preferred_element_type=F32)
            else:
                folded = nt(right_t, up_ref[l])
            fold_ref[2 * l + j] = halves(folded)

    for l in range(layers):
        h_loads[l].wait()
        g_loads[l].wait()
        for place in range(2):
            j = side if place else 1 - side
            both = nt(fold_ref[2 * l + j], pair_ref[l, 1 - place])
            mix_ref[l, place] = both[:m_right] + both[m_right:]
        if l == 0:


            @pl.when(behind > 0)
            def _():
                pl.semaphore_wait(row_sem, behind)

        for step in range(1, ncol):
            copy = col_copy(
                mix_ref.at[l, 1 - step % 2],
                mix_in_ref.at[step - 1, l],
                mix_ssem,
                mix_rsem.at[l],
                step,
            )
            copy.start()

    load(4 + 2 * layers, words_ref, words_ref).wait()
    unpack(0)
    def st_copy(l):
        return pltpu.make_async_remote_copy(
            src_ref=st_out_ref.at[l],
            dst_ref=st_in_ref.at[l],
            send_sem=st_ssem.at[l],
            recv_sem=st_rsem.at[l],
            device_id={"col": ic + 1 - 2 * side},
            device_id_type=MESH,
        )

    def join(l):
        st_copy(l).wait_recv()
        st = st_own_ref[l] + st_in_ref[l]
        st_high = st.astype(BF16)
        st_hi_ref[l] = st_high
        st_lo_ref[l] = (st - st_high.astype(F32)).astype(BF16)

    for n, (l, place) in enumerate(tasks):
        if n + 1 < len(tasks):
            unpack(n + 1)
        st = nt(signs_ref[n], pair_ref[l, place])
        if n >= layers:
            st_own_ref[l] = st
        else:
            st_out_ref[l] = st
        if n == layers - 1:
            for m in range(layers):
                st_copy(m).start()
    ps_ref[...] = jnp.zeros_like(ps_ref)

    length = len_ref[0]
    position = lax.broadcasted_iota(jnp.int32, (1, seq), 1)
    weights = jnp.where(position < length, 1.0, 0.0).astype(F32) / jnp.full(
        (1, seq), length, jnp.int32
    ).astype(F32)

    def block_copy(row, l, ssem):
        return pltpu.make_async_remote_copy(
            src_ref=sk_ref.at[l],
            dst_ref=rx_ref.at[ie, pair],
            send_sem=ssem,
            recv_sem=sk_rsem.at[ie],
            device_id={"ex": row, "col": 2 * l + side},
            device_id_type=MESH,
        )

    def other_row(i):
        up = i + jnp.where(i >= ie, 1, 0)
        down = nex - 1 - i - jnp.where(i >= nex - 1 - ie, 1, 0)
        return jnp.where(2 * ie < nex, down, up)

    for l in range(layers):
        passing(mix_in_ref.at[:, l], mix_rsem.at[l]).wait_recv()
        total = mix_ref[l, 1]
        for step in range(1, ncol):
            total = total + mix_in_ref[step - 1, l]
        left = halves(total * weights)
        join(l)
        out = nt(left, st_hi_ref[l]) + nt(left, st_lo_ref[l])
        sk_ref[l] = out[:m_right] + out[m_right:]

        if l == 0:

            @pl.when(ie < nex - 1)
            def _():
                pl.semaphore_wait(ready_sem, (nex - 1 - ie) * ncol)

        def send_row(i, l=l):
            block_copy(other_row(i), l, sk_ssem).start()

        repeat(nex - 1, send_row)

        @pl.when(pair != l)
        def _(l=l):
            block_copy(ie, l, own_ssem).start()

        @pl.when(pair == l)
        def _(l=l):
            pltpu.make_async_copy(sk_ref.at[l], rx_ref.at[ie, pair], sk_rsem.at[ie]).start()

    tg_load.wait()
    targets = tg_ref[...]
    high = targets.astype(BF16)
    t_ref[0:tpd] = high
    t_ref[tpd : 2 * tpd] = (targets - high.astype(F32)).astype(BF16)
    squares = targets * targets
    lanes = 128
    folded = squares[:, 0:lanes]
    for b in range(1, squares.shape[1] // lanes):
        folded = folded + squares[:, b * lanes : (b + 1) * lanes]
    sq_high = folded.astype(BF16)
    rest = folded - sq_high.astype(F32)
    sq_mid = rest.astype(BF16)
    sq_low = (rest - sq_mid.astype(F32)).astype(BF16)
    ones = jnp.ones((8, lanes), BF16)
    tsq = (nt(ones, sq_high) + nt(ones, sq_mid) + nt(ones, sq_low))[0:1]

    def placed(values):
        if groups == 1:
            return values
        where = lax.rem(ie, groups) * tpd
        place = (
            lax.broadcasted_iota(jnp.int32, (tpd, tpd * groups), 0) + where
            == lax.broadcasted_iota(jnp.int32, (tpd, tpd * groups), 1)
        ).astype(F32)
        return jnp.dot(values, place, precision=lax.Precision.HIGHEST, preferred_element_type=F32)

    tsq = placed(tsq)
    span = tsq.shape[1]
    for e in range(nex):
        ps_ref[e, 2:3, 0:span] = tsq

    goal = ie // groups
    slot = lax.rem(ie, groups) * ncol + ic

    def score_copy(e):
        return pltpu.make_async_remote_copy(
            src_ref=ps_ref.at[e],
            dst_ref=fin_ref.at[slot],
            send_sem=ps_ssem,
            recv_sem=fin_rsem,
            device_id={"ex": e, "col": goal},
            device_id_type=MESH,
        )

    def candidate(e):
        total = rx_ref[e, 0]
        for p in range(1, layers):
            total = total + rx_ref[e, p]
        return total

    def stays(e):
        return jnp.logical_and(e == ie, goal == ic)

    def score(e):
        passing(rx_ref.at[e], sk_rsem.at[e]).wait_recv()
        total = candidate(e)
        feats = jnp.concatenate([total[r : r + 1] for r in range(rows)], axis=1)
        part = nt(halves(feats), t_ref[...])
        part = part[0:1] + part[1:2]
        part = placed(part[:, 0:tpd] + part[:, tpd : 2 * tpd])
        squares = jnp.sum(jnp.sum(total * total, axis=1, keepdims=True), axis=0, keepdims=True)
        ps_ref[e, 0:1, 0:span] = part
        ps_ref[e, 1:2, :] = jnp.broadcast_to(squares, (1, 128))

        @pl.when(jnp.logical_not(stays(e)))
        def _():
            score_copy(e).start()

        @pl.when(stays(e))
        def _():
            pltpu.make_async_copy(ps_ref.at[e], fin_ref.at[slot], fin_rsem).start()

    repeat(nex, score)

    own = candidate(ie)
    passing(mix_in_ref, mix_ssem).wait_send()
    for l in range(layers):
        st_copy(l).wait_send()
    passing(rx_ref.at[0, 1:layers], own_ssem).wait_send()
    passing(rx_ref.at[1:nex], sk_ssem).wait_send()
    passing(fin_ref, fin_rsem).wait_recv()

    sums = fin_ref[0]
    for k in range(1, groups * ncol):
        sums = sums + fin_ref[k]
    csq = fin_ref[0, 1:2]
    for k in range(1, ncol):
        csq = csq + fin_ref[k, 1:2]
    t_scale = lax.rsqrt(sums[2:3] / cols + epsilon) / math.sqrt(cols)
    c_scale = lax.rsqrt(csq / cols + epsilon)
    own_scale = jnp.concatenate([c_scale] * (k_left // 128), axis=1)
    out_ref[0:rows] = own * own_scale
    out_ref[rows : rows + 1, 0:128] = sums[0:1] * t_scale * c_scale

    @pl.when(goal == ic)
    def _():
        passing(ps_ref.at[1:nex], ps_ssem).wait_send()

    @pl.when(goal != ic)
    def _():
        passing(ps_ref, ps_ssem).wait_send()


def spread(packed_ref, feat_ref, score_ref):
    rows = packed_ref.shape[0] // 2
    k_left = packed_ref.shape[1]
    for r in range(rows):
        feat_ref[:, r * k_left : (r + 1) * k_left] = packed_ref[r : r + 1]
    score_ref[...] = packed_ref[rows : rows + 1, 0 : score_ref.shape[1]]


def on_device(
    nex,
    ncol,
    hidden_input,
    output_gradient,
    lengths,
    adapter_down,
    adapter_up,
    left_sign_words,
    right_sign_words,
    targets,
):
    examples, layers, seq, width = hidden_input.shape
    right_by_column = jnp.swapaxes(right_sign_words, 2, 3)
    nwords = left_sign_words.shape[2]
    m_right = right_sign_words.shape[3]
    k_left = nwords * BITS
    tpd, own_cols = targets.shape
    rows = own_cols // k_left
    groups = nex // ncol
    assert examples == 1 and nex == groups * ncol and rows * k_left == own_cols
    assert rows == m_right and ncol == 2 * layers
    blocks = 2 * layers
    span = tpd * groups
    any_space = pl.BlockSpec(memory_space=pltpu.HBM)
    vmem = pl.BlockSpec(memory_space=pltpu.VMEM)
    peers = ncol - 1
    sems = pltpu.SemaphoreType.DMA
    packed = pl.pallas_call(
        functools.partial(kernel, nex, ncol, groups),
        out_shape=pltpu.VMEM((2 * rows, k_left), F32),
        in_specs=[any_space] * 2 + [pl.BlockSpec(memory_space=pltpu.SMEM)] + [any_space] * 5,
        out_specs=vmem,
        scratch_shapes=[
            pltpu.VMEM((layers, 2, seq, width), BF16),
            pltpu.VMEM(adapter_down.shape, BF16),
            pltpu.VMEM(adapter_up.shape, BF16),
            pltpu.VMEM(left_sign_words.shape, jnp.int32),
            pltpu.VMEM(right_by_column.shape, jnp.int32),
            pltpu.VMEM(targets.shape, F32),
            pltpu.VMEM((blocks, k_left, width), BF16),
            pltpu.VMEM((layers, k_left, seq), F32),
            pltpu.VMEM((layers, k_left, seq), F32),
            pltpu.VMEM((layers, k_left, seq), F32),
            pltpu.VMEM((layers, k_left, seq), BF16),
            pltpu.VMEM((layers, k_left, seq), BF16),
            pltpu.VMEM((2 * tpd, own_cols), BF16),
            pltpu.VMEM((blocks, 2 * m_right, width), BF16),
            pltpu.VMEM((layers, 2, m_right, seq), F32),
            pltpu.VMEM((peers, layers, m_right, seq), F32),
            pltpu.VMEM((layers, rows, k_left), F32),
            pltpu.VMEM((nex, layers, rows, k_left), F32),
            pltpu.VMEM((nex, 4, 128), F32),
            pltpu.VMEM((groups * ncol, 4, 128), F32),
            sems((5 + 2 * layers,)),
            pltpu.SemaphoreType.REGULAR,
            pltpu.SemaphoreType.REGULAR,
            sems,
            sems((layers,)),
            sems((layers,)),
            sems((layers,)),
            sems,
            sems,
            sems((nex,)),
            sems,
            sems,
        ],
        compiler_params=pltpu.CompilerParams(collective_id=0, has_side_effects=True),
    )(
        hidden_input,
        output_gradient,
        lengths,
        adapter_down,
        adapter_up,
        left_sign_words,
        right_by_column,
        targets,
    )
    return pl.pallas_call(
        spread,
        out_shape=(
            jax.ShapeDtypeStruct((1, own_cols), F32),
            jax.ShapeDtypeStruct((1, span), F32),
        ),
        in_specs=[vmem],
        out_specs=(vmem, vmem),
    )(pltpu.with_memory_space_constraint(packed, pltpu.VMEM))


def solution(mesh):
    return jax.shard_map(
        functools.partial(on_device, mesh.shape["ex"], mesh.shape["col"]),
        mesh=mesh,
        in_specs=(
            P(("grp", "ex"), None, None, "col"),
            P(("grp", "ex"), None, None, "col"),
            P(("grp", "ex")),
            P(None, None, "col"),
            P(None, "col", None),
            P(None, None, None, "col"),
            P(),
            P(("grp", "ex"), "col"),
        ),
        out_specs=(P(("grp", "ex"), "col"), P(("grp", "ex"), "col")),
        check_vma=False,
    )
```
